32 devices in a mesh: pipe: 4 (over y, x), expert: 8 (over z, core).
Axes of the slice: x: 2, y: 2, z: 4, core: 2. Of those that a mesh axis runs over, the one named last changes fastest.
Arguments:
- tokens_in: bfloat16 [4, 2048, 2048], P('pipe', 'expert'), may hold values from -6 to 6
- out_grad: bfloat16 [4, 2048, 2048], P('pipe', 'expert'), may hold values from -6 to 6
- route_weight: float32 [4, 2048, 8], P('pipe', 'expert'), may hold values from 0.05 to 1
- expert_ids: int32 [4, 2048, 8], P('pipe', 'expert'), may hold values from 0 to 127, as said below
- slot_pos: int32 [4, 2048, 8], P('pipe', 'expert'), may hold values from 0 to 19, as said below
- dropped: int32 [4, 2048, 8], P('pipe', 'expert'), may hold values from 0 to 1, as said below
- gate_weight: bfloat16 [4, 8, 2048, 384], P('pipe', 'expert'), may hold values from -0.125 to 0.125
- up_weight: bfloat16 [4, 8, 2048, 384], P('pipe', 'expert'), may hold values from -0.125 to 0.125
- down_weight: bfloat16 [4, 8, 384, 2048], P('pipe', 'expert'), may hold values from -0.3125 to 0.3125
Outputs:
- upstream: bfloat16 [4, 2048, 2048], P('pipe', 'expert')
- grad_gate: bfloat16 [4, 8, 2048, 384], P('pipe', 'expert')
- grad_up: bfloat16 [4, 8, 2048, 384], P('pipe', 'expert')
- grad_down: bfloat16 [4, 8, 384, 2048], P('pipe', 'expert')
The draws below stay inside these ranges and needn't reach their ends.
Inputs may be any that keep to these rules, and one draw needn't show every extreme that they name: `expert_ids`: each token names 8 different experts. A route's slot_pos counts the earlier routes (by token, then rank) to the same expert among the 256 tokens of its source block, capped at 19; in every layer some expert of the window gets 20 or more routes from every block. dropped is 1 exactly where that count reaches 20.
All inputs are finite; a program needn't handle non-finite values.
Results may differ from the reference program's by a relative error of at most 0.0058.
Values may be sent and summed in bfloat16 or wider, within the bound.
No kernel may reach another device: no remote copies, remote signals or barrier semaphores. Data moves between devices by JAX's collectives and lax.ppermute only.
A program may use at most 64 MiB of HBM per device.

```python
import math
import jax
import jax.numpy as jnp
from jax import lax

D = 2048
EXPERTS = 128
TOPK = 8
FW = 384
TOK_DEV = 256
CAP = 20
WIN_EXPERTS = 8
LAYERS = 4
TOKENS = 2048


def routing_tables(key):
    base = jax.random.fold_in(key, 7)
    key_noise, key_level, key_hot = jax.random.split(base, 3)
    noise = jax.random.randint(key_noise, (LAYERS, TOKENS, EXPERTS), 0, 1 << 16)
    level = jax.random.randint(key_level, (LAYERS, 1, EXPERTS), 0, 4)
    hot = jax.random.randint(key_hot, (LAYERS, 1, 1), 0, WIN_EXPERTS)
    labels = jnp.arange(EXPERTS).astype(jnp.int32)[None, None, :]
    even = (jnp.arange(TOKENS) % 2 == 0).astype(jnp.int32)[None, :, None]
    boost = (labels == hot).astype(jnp.int32) * even
    score = (noise + level * (1 << 15) + boost * (1 << 20)) * EXPERTS + labels
    picked = jax.lax.top_k(score, TOPK)[1].astype(jnp.int32)
    layer_idx = jnp.arange(LAYERS).astype(jnp.int32)[:, None, None]
    token_idx = jnp.arange(TOKENS).astype(jnp.int32)[None, :, None]
    counts = jnp.zeros((LAYERS, TOKENS, EXPERTS), jnp.int32).at[layer_idx, token_idx, picked].add(1)
    blocks = counts.reshape(LAYERS, TOKENS // TOK_DEV, TOK_DEV, EXPERTS)
    before = (jnp.cumsum(blocks, axis=2) - blocks).reshape(LAYERS, TOKENS, EXPERTS)
    rank = jnp.take_along_axis(before, picked, axis=2)
    return (picked, rank)


def draw_expert_ids(key, part):
    return routing_tables(key)[0]


def draw_slot_pos(key, part):
    rank = routing_tables(key)[1]
    return jnp.minimum(rank, CAP - 1).astype(jnp.int32)


def draw_dropped(key, part):
    rank = routing_tables(key)[1]
    return (rank >= CAP).astype(jnp.int32)


def block_levels(stream_key, shape, cuts, smallest, top_value):
    factor_of, own = 1.0, jax.random.fold_in(stream_key, 6)
    for position, blocks in cuts:
        draws = jnp.exp(jax.random.uniform(jax.random.fold_in(own, position), (blocks,), jnp.float32, smallest / len(cuts), top_value / len(cuts)))
        factor_of = factor_of * jnp.repeat(draws, shape[position] // blocks).reshape([-1 if axis == position else 1 for axis in range(len(shape))])
    return factor_of


def centred(rng, shape, scale, most, shards=(), held_as=jnp.bfloat16):
    level = block_levels(rng, shape, shards, -0.22, 0.18) if shards else 1.0
    result = jax.random.normal(rng, shape, jnp.float32) * scale * level
    return jnp.minimum(jnp.maximum(result, -most), most).astype(held_as)


def setup_inputs(seed: int = 0) -> dict:
    key_list = jax.random.split(jax.random.key(seed), 10)
    return {
        "tokens_in": centred(key_list[0], (LAYERS, TOKENS, D), 1.0, 6.0, ((0, 4), (1, 8))),
        "out_grad": centred(key_list[1], (LAYERS, TOKENS, D), 1.0, 6.0, ((0, 4), (1, 8))),
        "route_weight": jnp.clip(jnp.exp(math.log(1.0) - 2.9957323 * jax.random.uniform(key_list[2], (LAYERS, TOKENS, TOPK), jnp.float32) ** block_levels(key_list[2], (LAYERS, TOKENS, TOPK), ((0, 4), (1, 8)), -0.2, 0.2)), 0.05, 1.0),
        "expert_ids": draw_expert_ids(jax.random.fold_in(key_list[9], 71), 0),
        "slot_pos": draw_slot_pos(jax.random.fold_in(key_list[9], 71), 0),
        "dropped": draw_dropped(jax.random.fold_in(key_list[9], 71), 0),
        "gate_weight": centred(key_list[6], (LAYERS, WIN_EXPERTS, D, FW), D ** -0.5, 0.125, ((0, 4), (1, 8))),
        "up_weight": centred(key_list[7], (LAYERS, WIN_EXPERTS, D, FW), D ** -0.5, 0.125, ((0, 4), (1, 8))),
        "down_weight": centred(key_list[8], (LAYERS, WIN_EXPERTS, FW, D), FW ** -0.5, 0.3125, ((0, 4), (1, 8))),
    }


def expert_rows(expert_in, expert_grad, w_gate, w_up, w_down):
    gate_pre = jnp.dot(expert_in, w_gate, preferred_element_type=jnp.float32)
    up_pre = jnp.dot(expert_in, w_up, preferred_element_type=jnp.float32)
    sigma = jax.nn.sigmoid(gate_pre)
    active = gate_pre * sigma
    hidden = (active * up_pre).astype(jnp.bfloat16)
    hidden_grad = lax.dot_general(expert_grad, w_down, (((1,), (1,)), ((), ())), preferred_element_type=jnp.float32)
    gate_grad = (hidden_grad * up_pre * sigma * (1.0 + gate_pre * (1.0 - sigma))).astype(jnp.bfloat16)
    up_grad = (hidden_grad * active).astype(jnp.bfloat16)
    row_grad = lax.dot_general(gate_grad, w_gate, (((1,), (1,)), ((), ())), preferred_element_type=jnp.float32)
    row_grad = row_grad + lax.dot_general(up_grad, w_up, (((1,), (1,)), ((), ())), preferred_element_type=jnp.float32)
    contract = (((0,), (0,)), ((), ()))
    grad_gate = lax.dot_general(expert_in, gate_grad, contract, preferred_element_type=jnp.float32).astype(jnp.bfloat16)
    grad_up = lax.dot_general(expert_in, up_grad, contract, preferred_element_type=jnp.float32).astype(jnp.bfloat16)
    grad_down = lax.dot_general(hidden, expert_grad, contract, preferred_element_type=jnp.float32).astype(jnp.bfloat16)
    return row_grad.astype(jnp.bfloat16), grad_gate, grad_up, grad_down


def one_layer(args):
    tokens_in, out_grad, route_weight, expert_ids, slot_pos, dropped, w_gate, w_up, w_down = args
    rows = WIN_EXPERTS * CAP
    source = (jnp.arange(TOKENS) // TOK_DEV).astype(jnp.int32)
    live = (expert_ids < WIN_EXPERTS) & (dropped == 0)
    where_row = jnp.where(live, expert_ids * rows + source[:, None] * CAP + slot_pos, WIN_EXPERTS * rows).astype(jnp.int32)
    token_index = jnp.broadcast_to(jnp.arange(TOKENS).astype(jnp.int32)[:, None], (TOKENS, TOPK))
    token_at = jnp.full((WIN_EXPERTS * rows,), TOKENS, jnp.int32).at[where_row.reshape(-1)].set(token_index.reshape(-1), mode="drop")
    weight_at = jnp.zeros((WIN_EXPERTS * rows,), jnp.float32).at[where_row.reshape(-1)].set(route_weight.reshape(-1), mode="drop")
    pad_in = jnp.concatenate([tokens_in, jnp.zeros((1, D), jnp.bfloat16)], axis=0)
    pad_grad = jnp.concatenate([out_grad, jnp.zeros((1, D), jnp.bfloat16)], axis=0)
    expert_in = pad_in[token_at].reshape(WIN_EXPERTS, rows, D)
    expert_grad = (weight_at[:, None] * pad_grad[token_at].astype(jnp.float32)).astype(jnp.bfloat16).reshape(WIN_EXPERTS, rows, D)
    row_grad, grad_gate, grad_up, grad_down = lax.map(lambda a: expert_rows(*a), (expert_in, expert_grad, w_gate, w_up, w_down))
    summed = jnp.zeros((TOKENS + 1, D), jnp.float32).at[token_at].add(row_grad.reshape(WIN_EXPERTS * rows, D).astype(jnp.float32))
    section_grad = (out_grad.astype(jnp.float32) + summed[:TOKENS]).astype(jnp.bfloat16)
    return section_grad, grad_gate, grad_up, grad_down


def reference(tokens_in, out_grad, route_weight, expert_ids, slot_pos, dropped, gate_weight, up_weight, down_weight):
    section_grad, grad_gate, grad_up, grad_down = lax.map(one_layer, (tokens_in, out_grad, route_weight, expert_ids, slot_pos, dropped, gate_weight, up_weight, down_weight))
    upstream = jnp.concatenate([section_grad[1:], jnp.zeros((1, TOKENS, D), jnp.bfloat16)], axis=0)
    return upstream, grad_gate, grad_up, grad_down
```

```python
import functools

import jax
import jax.numpy as jnp
from jax import lax
from jax.experimental import pallas as pl
from jax.experimental.pallas import tpu as pltpu
from jax.sharding import PartitionSpec as P

CAP = 20
PAIR = 2 * CAP
F32 = jnp.float32
BF16 = jnp.bfloat16


def vmem(count):
    return [pl.BlockSpec(memory_space=pltpu.VMEM)] * count


def is_first(shape):
    return lax.rem(lax.broadcasted_iota(jnp.int32, shape, 0), PAIR) < CAP


def match_rows(keys, first_row, rows):
    tokens = keys.shape[1]
    row = lax.broadcasted_iota(jnp.int32, (rows, tokens), 0)
    slot = first_row + row - jnp.where(lax.rem(row, PAIR) < CAP, 0, CAP)
    return [keys[k : k + 1, :] == slot for k in range(keys.shape[0])]


def gather_kernel(keys_ref, weight_ref, in_ref, grad_ref, *outs):
    keys = keys_ref[...]
    weight = weight_ref[...]
    rows = PAIR * len(outs)
    tokens = keys.shape[1]
    own = jnp.zeros((rows, tokens), F32)
    scaled = jnp.zeros((rows, tokens), F32)
    for k, hit in enumerate(match_rows(keys, 0, rows)):
        own = jnp.where(hit, 1.0, own)
        scaled = jnp.where(hit, weight[k : k + 1, :], scaled)
    first = is_first((rows, tokens))
    pick_in = jnp.where(first, own, 0.0).astype(BF16)
    pick_grad = jnp.where(first, 0.0, own).astype(BF16)
    row_weight = jnp.sum(scaled, axis=1, keepdims=True)
    got = jnp.dot(pick_in, in_ref[...], preferred_element_type=F32)
    got = got + row_weight * jnp.dot(pick_grad, grad_ref[...], preferred_element_type=F32)
    got = got.astype(BF16)
    for k, out in enumerate(outs):
        out[...] = got[k * PAIR : (k + 1) * PAIR, :]


def gather(keys, weight, inputs, grads, count):
    width = inputs.shape[1]
    return pl.pallas_call(
        gather_kernel,
        out_shape=[jax.ShapeDtypeStruct((PAIR, width), BF16)] * count,
        in_specs=vmem(4),
        out_specs=vmem(count),
        name="gather",
    )(keys, weight, inputs, grads)


def nt(a, b):
    return lax.dot_general(a, b, (((1,), (1,)), ((), ())), preferred_element_type=F32)


def tn(a, b):
    return lax.dot_general(a, b, (((0,), (0,)), ((), ())), preferred_element_type=F32)


def expert_kernel(count, *refs):
    payloads = refs[:count]
    w_gate, w_up, w_down = refs[count : count + 3]
    returns = refs[count + 3 : 2 * count + 3]
    gate_out, up_out, hidden_out = refs[2 * count + 3 :]
    rows = count * PAIR
    half = w_gate.shape[0] // 2
    both = jnp.concatenate([p[...] for p in payloads], axis=0)
    gate_pre = jnp.dot(both, w_gate[...], preferred_element_type=F32)
    up_pre = jnp.dot(both, w_up[...], preferred_element_type=F32)
    hidden_grad = pltpu.roll(nt(both, w_down[...]), rows - CAP, 0)
    first = is_first(gate_pre.shape)
    sigma = jax.nn.sigmoid(gate_pre)
    active = gate_pre * sigma
    hidden = jnp.where(first, active * up_pre, 0.0)
    gate_grad = hidden_grad * up_pre * sigma * (1.0 + gate_pre * (1.0 - sigma))
    gate_grad = jnp.where(first, gate_grad, 0.0)
    up_grad = jnp.where(first, hidden_grad * active, 0.0)
    gate_out[...] = gate_grad.astype(BF16)
    up_out[...] = up_grad.astype(BF16)
    hidden_out[...] = pltpu.roll(hidden, CAP, 0).astype(BF16)
    gate_two = (gate_grad + pltpu.roll(gate_grad, CAP, 0)).astype(BF16)
    up_two = (up_grad + pltpu.roll(up_grad, CAP, 0)).astype(BF16)
    left = nt(gate_two, w_gate[:half, :]) + nt(up_two, w_up[:half, :])
    right = nt(gate_two, w_gate[half:, :]) + nt(up_two, w_up[half:, :])
    row_grad = jnp.where(is_first(left.shape), left, right).astype(BF16)
    for k, out in enumerate(returns):
        out[...] = row_grad[k * PAIR : (k + 1) * PAIR, :]


def expert_chunk(payloads, w_gate, w_up, w_down):
    count = len(payloads)
    width, hidden = w_gate.shape
    out = pl.pallas_call(
        functools.partial(expert_kernel, count),
        out_shape=[jax.ShapeDtypeStruct((PAIR, width // 2), BF16)] * count
        + [jax.ShapeDtypeStruct((PAIR * count, hidden), BF16)] * 3,
        in_specs=vmem(count + 3),
        out_specs=vmem(count + 3),
        name="expert",
    )(*payloads, w_gate, w_up, w_down)
    return out[:count], out[count:]


def weight_kernel(count, chunks, *refs):
    payloads = refs[:count]
    small = refs[count : count + 3 * chunks]
    grad_gate, grad_up, grad_down = refs[count + 3 * chunks :]
    both = jnp.concatenate([p[...] for p in payloads], axis=0)
    gate = jnp.concatenate([r[...] for r in small[0::3]], axis=0)
    up = jnp.concatenate([r[...] for r in small[1::3]], axis=0)
    hidden = jnp.concatenate([r[...] for r in small[2::3]], axis=0)
    grad_gate[...] = tn(both, gate).astype(BF16)
    grad_up[...] = tn(both, up).astype(BF16)
    grad_down[...] = tn(hidden, both).astype(BF16)


def weight_grads(payloads, small, width, hidden):
    count = len(payloads)
    chunks = len(small)
    flat = [a for part in small for a in part]
    return pl.pallas_call(
        functools.partial(weight_kernel, count, chunks),
        out_shape=[
            jax.ShapeDtypeStruct((width, hidden), BF16),
            jax.ShapeDtypeStruct((width, hidden), BF16),
            jax.ShapeDtypeStruct((hidden, width), BF16),
        ],
        in_specs=vmem(count + 3 * chunks),
        out_specs=vmem(3),
        name="weight_grads",
    )(*payloads, *flat)


def combine_kernel(keys_ref, grad_ref, *refs):
    returned, out = refs[:-1], refs[-1]
    keys = keys_ref[...]
    rows = PAIR * len(returned)
    tokens = keys.shape[1]
    half = grad_ref.shape[1] // 2
    own = jnp.zeros((rows, tokens), F32)
    for hit in match_rows(keys, 0, rows):
        own = jnp.where(hit, 1.0, own)
    first = is_first((rows, tokens))
    back = jnp.concatenate([r[...] for r in returned], axis=0)
    for side in range(2):
        pick = jnp.where(first, own, 0.0) if side == 0 else jnp.where(first, 0.0, own)
        cols = slice(side * half, (side + 1) * half)
        total = grad_ref[:, cols].astype(F32) + tn(pick.astype(BF16), back)
        out[:, cols] = total.astype(BF16)


def combine(keys, grads, returned):
    return pl.pallas_call(
        combine_kernel,
        out_shape=jax.ShapeDtypeStruct(grads.shape, BF16),
        in_specs=vmem(2 + len(returned)),
        out_specs=pl.BlockSpec(memory_space=pltpu.VMEM),
        name="combine",
    )(keys, grads, *returned)


def per_device(
    tokens_in,
    out_grad,
    route_weight,
    expert_ids,
    slot_pos,
    dropped,
    gate_weight,
    up_weight,
    down_weight,
):
    inputs = tokens_in[0]
    grads = out_grad[0]
    w_gate = gate_weight[0, 0]
    w_up = up_weight[0, 0]
    w_down = down_weight[0, 0]
    width, hidden = w_gate.shape
    n_expert = lax.axis_size("expert")
    n_pipe = lax.axis_size("pipe")
    me = lax.axis_index("expert")
    both_axes = ("pipe", "expert")

    def to_partner(value, k):
        return lax.ppermute(value, "expert", [(i, i ^ k) for i in range(n_expert)])

    def to_before(value, k):
        pairs = [
            (p * n_expert + i, (p - 1) * n_expert + (i ^ k))
            for p in range(1, n_pipe)
            for i in range(n_expert)
        ]
        return lax.ppermute(value, both_axes, pairs)

    live = (expert_ids[0] < n_expert) & (dropped[0] == 0)
    key = jnp.where(live, (expert_ids[0] ^ me) * PAIR + slot_pos[0], -1)
    keys = jnp.transpose(key)
    weight = jnp.transpose(route_weight[0])
    sent = gather(keys, weight, inputs, grads, n_expert)

    near = list(range(n_expert // 2))
    far_a = list(range(n_expert // 2, 3 * n_expert // 4))
    far_b = list(range(3 * n_expert // 4, n_expert))
    got = {}
    for k in far_a + far_b + near[::-1]:
        got[k] = to_partner(sent[k], k) if k else sent[k]
    next_grads = to_before(grads, 0)
    next_keys = to_before(keys, 0)

    returned = {}
    order, small = [], []
    for chunk in (far_a, near, far_b):
        back, parts = expert_chunk([got[k] for k in chunk], w_gate, w_up, w_down)
        for k, value in zip(chunk, back):
            returned[k] = to_before(value, k)
        order += chunk
        small.append(parts)
    grad_gate, grad_up, grad_down = weight_grads([got[k] for k in order], small, width, hidden)
    upstream = combine(next_keys, next_grads, [returned[k] for k in range(n_expert)])
    return (upstream[None], grad_gate[None, None], grad_up[None, None], grad_down[None, None])


def solution(mesh):
    return jax.shard_map(
        per_device,
        mesh=mesh,
        in_specs=(
            P("pipe", "expert", None),
            P("pipe", "expert", None),
            P("pipe", "expert", None),
            P("pipe", "expert", None),
            P("pipe", "expert", None),
            P("pipe", "expert", None),
            P("pipe", "expert", None, None),
            P("pipe", "expert", None, None),
            P("pipe", "expert", None, None),
        ),
        out_specs=(
            P("pipe", "expert", None),
            P("pipe", "expert", None, None),
            P("pipe", "expert", None, None),
            P("pipe", "expert", None, None),
        ),
        check_vma=False,
    )
```

```python
import functools

import jax
import jax.numpy as jnp
from jax import lax
from jax.experimental import pallas as pl
from jax.experimental.pallas import tpu as pltpu
from jax.sharding import PartitionSpec as P

CAP = 20
PAIR = 2 * CAP
F32 = jnp.float32
BF16 = jnp.bfloat16
SHORT = pl.CostEstimate(flops=1, transcendentals=0, bytes_accessed=1)


def vmem(count):
    return [pl.BlockSpec(memory_space=pltpu.VMEM)] * count


def is_first(shape):
    return lax.rem(lax.broadcasted_iota(jnp.int32, shape, 0), PAIR) < CAP


def match_rows(keys, first_row, rows):
    tokens = keys.shape[1]
    row = lax.broadcasted_iota(jnp.int32, (rows, tokens), 0)
    slot = first_row + row - jnp.where(lax.rem(row, PAIR) < CAP, 0, CAP)
    return [keys[k : k + 1, :] == slot for k in range(keys.shape[0])]


def gather_kernel(keys_ref, weight_ref, in_ref, grad_ref, *outs):
    keys = keys_ref[...]
    weight = weight_ref[...]
    rows = sum(out.shape[0] for out in outs)
    tokens = keys.shape[1]
    own = jnp.zeros((rows, tokens), F32)
    scaled = jnp.zeros((rows, tokens), F32)
    for k, hit in enumerate(match_rows(keys, 0, rows)):
        own = jnp.where(hit, 1.0, own)
        scaled = jnp.where(hit, weight[k : k + 1, :], scaled)
    first = is_first((rows, tokens))
    pick_in = jnp.where(first, own, 0.0).astype(BF16)
    pick_grad = jnp.where(first, 0.0, own).astype(BF16)
    row_weight = jnp.sum(scaled, axis=1, keepdims=True)
    got = jnp.dot(pick_in, in_ref[...], preferred_element_type=F32)
    got = got + row_weight * jnp.dot(pick_grad, grad_ref[...], preferred_element_type=F32)
    got = got.astype(BF16)
    start = 0
    for out in outs:
        out[...] = got[start : start + out.shape[0], :]
        start += out.shape[0]


def gather(keys, weight, inputs, grads, chips, apart):
    width = inputs.shape[1]
    sizes = [n for c in range(chips) for n in ([PAIR, PAIR] if c in apart else [2 * PAIR])]
    outs = pl.pallas_call(
        gather_kernel,
        out_shape=[jax.ShapeDtypeStruct((n, width), BF16) for n in sizes],
        in_specs=vmem(4),
        out_specs=vmem(len(sizes)),
        name="gather",
        compiler_params=pltpu.CompilerParams(vmem_limit_bytes=16 << 20),
        cost_estimate=SHORT,
    )(keys, weight, inputs, grads)
    outs = list(outs)
    return [[outs.pop(0), outs.pop(0)] if c in apart else outs.pop(0) for c in range(chips)]


def nt(a, b):
    return lax.dot_general(a, b, (((1,), (1,)), ((), ())), preferred_element_type=F32)


def tn(a, b):
    return lax.dot_general(a, b, (((0,), (0,)), ((), ())), preferred_element_type=F32)


def joined(pieces):
    return jnp.concatenate(
        [
            p[PAIR : 2 * PAIR, :] if i % 2 and p.shape[0] > PAIR else p[:PAIR, :]
            for i, p in enumerate(pieces)
        ],
        axis=0,
    )


def expert_kernel(count, with_keys, *refs):
    if with_keys:
        keys_ref, refs = refs[0], refs[1:]
    payloads = refs[:count]
    w_gate, w_up, w_down = refs[count : count + 3]
    returns = refs[count + 3 : -3]
    gate_out, up_out, hidden_out = refs[-3:]
    rows = count * PAIR
    half = w_gate.shape[0] // 2
    both = joined(payloads)
    gate_pre = jnp.dot(both, w_gate[...], preferred_element_type=F32)
    up_pre = jnp.dot(both, w_up[...], preferred_element_type=F32)
    hidden_grad = pltpu.roll(nt(both, w_down[...]), rows - CAP, 0)
    first = is_first(gate_pre.shape)
    sigma = jax.nn.sigmoid(gate_pre)
    active = gate_pre * sigma
    hidden = jnp.where(first, active * up_pre, 0.0)
    gate_grad = hidden_grad * up_pre * sigma * (1.0 + gate_pre * (1.0 - sigma))
    gate_grad = jnp.where(first, gate_grad, 0.0)
    up_grad = jnp.where(first, hidden_grad * active, 0.0)
    gate_out[...] = gate_grad.astype(BF16)
    up_out[...] = up_grad.astype(BF16)
    hidden_out[...] = pltpu.roll(hidden, CAP, 0).astype(BF16)
    gate_two = (gate_grad + pltpu.roll(gate_grad, CAP, 0)).astype(BF16)
    up_two = (up_grad + pltpu.roll(up_grad, CAP, 0)).astype(BF16)
    left = nt(gate_two, w_gate[:half, :]) + nt(up_two, w_up[:half, :])
    right = nt(gate_two, w_gate[half:, :]) + nt(up_two, w_up[half:, :])
    row_grad = jnp.where(is_first(left.shape), left, right).astype(BF16)
    step = rows // len(returns)
    for k, out in enumerate(returns):
        out[:step, :] = row_grad[k * step : (k + 1) * step, :]
    if with_keys:
        ranks, tokens = keys_ref.shape
        keys = keys_ref[...].astype(F32)
        block = jnp.floor((keys + 0.5) / PAIR)
        returns[0][2 * PAIR :, :tokens] = block.astype(BF16)
        returns[0][2 * PAIR :, tokens : 2 * tokens] = (keys - PAIR * block).astype(BF16)
        returns[0][2 * PAIR :, 2 * tokens :] = jnp.zeros((ranks, half - 2 * tokens), BF16)


def expert_chunk(pieces, w_gate, w_up, w_down, keys=None, single=False):
    count = len(pieces)
    width, hidden = w_gate.shape
    extra = [] if keys is None else [keys]
    rows = [PAIR] * count if single else [2 * PAIR] * (count // 2)
    if extra:
        rows[0] += keys.shape[0]
    out = pl.pallas_call(
        functools.partial(expert_kernel, count, bool(extra)),
        out_shape=[jax.ShapeDtypeStruct((r, width // 2), BF16) for r in rows]
        + [jax.ShapeDtypeStruct((PAIR * count, hidden), BF16)] * 3,
        in_specs=vmem(len(extra) + count + 3),
        out_specs=vmem(len(rows) + 3),
        name="expert",
        compiler_params=pltpu.CompilerParams(vmem_limit_bytes=20 << 20),
        cost_estimate=SHORT,
    )(*extra, *pieces, w_gate, w_up, w_down)
    return out[: len(rows)], out[len(rows) :]


def weight_kernel(count, chunks, *refs):
    payloads = refs[:count]
    small = refs[count : count + 3 * chunks]
    grad_gate, grad_up, grad_down = refs[count + 3 * chunks :]
    both = joined(payloads)
    gate = jnp.concatenate([r[...] for r in small[0::3]], axis=0)
    up = jnp.concatenate([r[...] for r in small[1::3]], axis=0)
    hidden = jnp.concatenate([r[...] for r in small[2::3]], axis=0)
    grad_gate[...] = tn(both, gate).astype(BF16)
    grad_up[...] = tn(both, up).astype(BF16)
    grad_down[...] = tn(hidden, both).astype(BF16)


def weight_grads(payloads, small, width, hidden):
    count = len(payloads)
    chunks = len(small)
    flat = [a for part in small for a in part]
    return pl.pallas_call(
        functools.partial(weight_kernel, count, chunks),
        out_shape=[
            jax.ShapeDtypeStruct((width, hidden), BF16),
            jax.ShapeDtypeStruct((width, hidden), BF16),
            jax.ShapeDtypeStruct((hidden, width), BF16),
        ],
        in_specs=vmem(count + 3 * chunks),
        out_specs=vmem(3),
        name="weight_grads",
        compiler_params=pltpu.CompilerParams(vmem_limit_bytes=24 << 20),
        cost_estimate=SHORT,
    )(*payloads, *flat)


def combine_kernel(ranks, grad_ref, *refs):
    returned, out = refs[:-1], refs[-1]
    rows = PAIR * len(returned)
    tokens = grad_ref.shape[0]
    block = returned[0][2 * PAIR : 2 * PAIR + ranks, :tokens].astype(F32)
    slot = returned[0][2 * PAIR : 2 * PAIR + ranks, tokens : 2 * tokens].astype(F32)
    keys = (PAIR * block + slot).astype(jnp.int32)
    half = grad_ref.shape[1] // 2
    own = jnp.zeros((rows, tokens), F32)
    for hit in match_rows(keys, 0, rows):
        own = jnp.where(hit, 1.0, own)
    first = is_first((rows, tokens))
    back = joined(returned)
    for side in range(2):
        pick = jnp.where(first, own, 0.0) if side == 0 else jnp.where(first, 0.0, own)
        cols = slice(side * half, (side + 1) * half)
        total = grad_ref[:, cols].astype(F32) + tn(pick.astype(BF16), back)
        out[:, cols] = total.astype(BF16)


def combine(ranks, grads, returned):
    return pl.pallas_call(
        functools.partial(combine_kernel, ranks),
        out_shape=jax.ShapeDtypeStruct(grads.shape, BF16),
        in_specs=vmem(1 + len(returned)),
        out_specs=pl.BlockSpec(memory_space=pltpu.VMEM),
        name="combine",
        compiler_params=pltpu.CompilerParams(vmem_limit_bytes=16 << 20),
        cost_estimate=SHORT,
    )(grads, *returned)


def per_device(
    tokens_in,
    out_grad,
    route_weight,
    expert_ids,
    slot_pos,
    dropped,
    gate_weight,
    up_weight,
    down_weight,
):
    inputs = tokens_in[0]
    grads = out_grad[0]
    w_gate = gate_weight[0, 0]
    w_up = up_weight[0, 0]
    w_down = down_weight[0, 0]
    width, hidden = w_gate.shape
    n_expert = lax.axis_size("expert")
    n_pipe = lax.axis_size("pipe")
    me = lax.axis_index("expert")
    both_axes = ("pipe", "expert")

    def to_partner(value, k):
        return lax.ppermute(value, "expert", [(i, i ^ k) for i in range(n_expert)])

    def to_before(value, k):
        pairs = [
            (p * n_expert + i, (p - 1) * n_expert + (i ^ k))
            for p in range(1, n_pipe)
            for i in range(n_expert)
        ]
        return lax.ppermute(value, both_axes, pairs)

    live = (expert_ids[0] < n_expert) & (dropped[0] == 0)
    key = jnp.where(live, (expert_ids[0] ^ me) * PAIR + slot_pos[0], -1)
    keys = jnp.transpose(key)
    weight = jnp.transpose(route_weight[0])
    chips = n_expert // 2
    near = list(range(1, chips // 2))
    early = list(range(chips // 2, 3 * chips // 4))
    late = list(range(3 * chips // 4, chips))
    sent = gather(keys, weight, inputs, grads, chips, [])
    behind, _ = lax.optimization_barrier((grads, sent[0]))
    next_grads = to_before(behind, 0)

    got, small, order, arrived, returned = {}, [], [], {}, {}

    def after(values, event):
        return lax.optimization_barrier((values, event))[0]

    def process(chunk, event=None, **options):
        pieces = [piece for c in chunk for piece in got[c]]
        if event is not None:
            pieces = after(pieces, event)
        back, parts = expert_chunk(pieces, w_gate, w_up, w_down, **options)
        order.extend(pieces)
        small.append(parts)
        return back, parts

    def forward(values, event):
        values = after(values, event)
        return [[value, to_partner(value, 1)] for value in values]

    for c in early + near:
        arrived[c] = to_partner(sent[c], 2 * c)
    got[0] = [sent[0], to_partner(sent[0], 1)]
    back, own = process([0], keys=keys)
    returned[0] = to_before(back[0], 0)
    for c, value in zip(late, after([sent[c] for c in late], own)):
        arrived[c] = to_partner(value, 2 * c)
    got.update(zip(early + near, forward([arrived[c] for c in early + near], own)))
    parts = own
    for chunk in (early, near):
        if chunk:
            back, parts = process(chunk, parts)
            for c, value in zip(chunk, back):
                returned[c] = to_before(value, 2 * c)
    got.update(zip(late, forward([arrived[c] for c in late], parts)))
    back, parts = process(late, single=True)
    for i, c in enumerate(late):
        returned[c] = [to_before(back[2 * i + j], 2 * c + j) for j in range(2)]
    grad_gate, grad_up, grad_down = weight_grads(order, small, width, hidden)
    both = [0] + early + near
    returned.update(zip(both, forward([returned[c] for c in both], grad_gate)))
    upstream = combine(
        keys.shape[0], next_grads, [piece for c in range(chips) for piece in returned[c]]
    )
    return (upstream[None], grad_gate[None, None], grad_up[None, None], grad_down[None, None])


def solution(mesh):
    return jax.shard_map(
        per_device,
        mesh=mesh,
        in_specs=(
            P("pipe", "expert", None),
            P("pipe", "expert", None),
            P("pipe", "expert", None),
            P("pipe", "expert", None),
            P("pipe", "expert", None),
            P("pipe", "expert", None),
            P("pipe", "expert", None, None),
            P("pipe", "expert", None, None),
            P("pipe", "expert", None, None),
        ),
        out_specs=(
            P("pipe", "expert", None),
            P("pipe", "expert", None, None),
            P("pipe", "expert", None, None),
            P("pipe", "expert", None, None),
        ),
        check_vma=False,
    )
```

```python
import functools

import jax
import jax.numpy as jnp
from jax import lax
from jax.experimental import pallas as pl
from jax.experimental.pallas import tpu as pltpu
from jax.sharding import PartitionSpec as P

CAP = 20
PAIR = 2 * CAP
F32 = jnp.float32
BF16 = jnp.bfloat16
SHORT = pl.CostEstimate(flops=1, transcendentals=0, bytes_accessed=1)


def vmem(count):
    return [pl.BlockSpec(memory_space=pltpu.VMEM)] * count


def is_first(shape):
    return lax.rem(lax.broadcasted_iota(jnp.int32, shape, 0), PAIR) < CAP


def match_rows(keys, first_row, rows):
    tokens = keys.shape[1]
    row = lax.broadcasted_iota(jnp.int32, (rows, tokens), 0)
    slot = first_row + row - jnp.where(lax.rem(row, PAIR) < CAP, 0, CAP)
    return [keys[k : k + 1, :] == slot for k in range(keys.shape[0])]


def gather_kernel(keys_ref, weight_ref, in_ref, grad_ref, *outs):
    keys = keys_ref[...]
    weight = weight_ref[...]
    rows = sum(out.shape[0] for out in outs)
    tokens = keys.shape[1]
    own = jnp.zeros((rows, tokens), F32)
    scaled = jnp.zeros((rows, tokens), F32)
    for k, hit in enumerate(match_rows(keys, 0, rows)):
        own = jnp.where(hit, 1.0, own)
        scaled = jnp.where(hit, weight[k : k + 1, :], scaled)
    first = is_first((rows, tokens))
    pick_in = jnp.where(first, own, 0.0).astype(BF16)
    pick_grad = jnp.where(first, 0.0, own).astype(BF16)
    row_weight = jnp.sum(scaled, axis=1, keepdims=True)
    got = jnp.dot(pick_in, in_ref[...], preferred_element_type=F32)
    got = got + row_weight * jnp.dot(pick_grad, grad_ref[...], preferred_element_type=F32)
    got = got.astype(BF16)
    start = 0
    for out in outs:
        out[...] = got[start : start + out.shape[0], :]
        start += out.shape[0]


def gather(keys, weight, inputs, grads, chips, apart):
    width = inputs.shape[1]
    sizes = [n for c in range(chips) for n in ([PAIR, PAIR] if c in apart else [2 * PAIR])]
    outs = pl.pallas_call(
        gather_kernel,
        out_shape=[jax.ShapeDtypeStruct((n, width), BF16) for n in sizes],
        in_specs=vmem(4),
        out_specs=vmem(len(sizes)),
        name="gather",
        compiler_params=pltpu.CompilerParams(vmem_limit_bytes=16 << 20),
        cost_estimate=SHORT,
    )(keys, weight, inputs, grads)
    outs = list(outs)
    return [[outs.pop(0), outs.pop(0)] if c in apart else outs.pop(0) for c in range(chips)]


def nt(a, b):
    return lax.dot_general(a, b, (((1,), (1,)), ((), ())), preferred_element_type=F32)


def tn(a, b):
    return lax.dot_general(a, b, (((0,), (0,)), ((), ())), preferred_element_type=F32)


def joined(refs, spans):
    return jnp.concatenate([r[lo:hi, :] for r, (lo, hi) in zip(refs, spans)], axis=0)


def expert_kernel(spans, with_keys, *refs):
    count = len(spans)
    if with_keys:
        keys_ref, refs = refs[0], refs[1:]
    payloads = refs[:count]
    w_gate, w_up, w_down = refs[count : count + 3]
    returns = refs[count + 3 : -3]
    gate_out, up_out, hidden_out = refs[-3:]
    rows = sum(hi - lo for lo, hi in spans)
    half = w_gate.shape[0] // 2
    both = joined(payloads, spans)
    gate_pre = jnp.dot(both, w_gate[...], preferred_element_type=F32)
    up_pre = jnp.dot(both, w_up[...], preferred_element_type=F32)
    hidden_grad = pltpu.roll(nt(both, w_down[...]), rows - CAP, 0)
    first = is_first(gate_pre.shape)
    sigma = jax.nn.sigmoid(gate_pre)
    active = gate_pre * sigma
    hidden = jnp.where(first, active * up_pre, 0.0)
    gate_grad = hidden_grad * up_pre * sigma * (1.0 + gate_pre * (1.0 - sigma))
    gate_grad = jnp.where(first, gate_grad, 0.0)
    up_grad = jnp.where(first, hidden_grad * active, 0.0)
    gate_out[...] = gate_grad.astype(BF16)
    up_out[...] = up_grad.astype(BF16)
    hidden_out[...] = pltpu.roll(hidden, CAP, 0).astype(BF16)
    gate_two = (gate_grad + pltpu.roll(gate_grad, CAP, 0)).astype(BF16)
    up_two = (up_grad + pltpu.roll(up_grad, CAP, 0)).astype(BF16)
    left = nt(gate_two, w_gate[:half, :]) + nt(up_two, w_up[:half, :])
    right = nt(gate_two, w_gate[half:, :]) + nt(up_two, w_up[half:, :])
    row_grad = jnp.where(is_first(left.shape), left, right).astype(BF16)
    step = rows // len(returns)
    for k, out in enumerate(returns):
        out[:step, :] = row_grad[k * step : (k + 1) * step, :]
    if with_keys:
        ranks, tokens = keys_ref.shape
        keys = keys_ref[...].astype(F32)
        block = jnp.floor((keys + 0.5) / PAIR)
        for out in returns:
            out[2 * PAIR :, :tokens] = block.astype(BF16)
            out[2 * PAIR :, tokens : 2 * tokens] = (keys - PAIR * block).astype(BF16)
            out[2 * PAIR :, 2 * tokens :] = jnp.zeros((ranks, half - 2 * tokens), BF16)


def expert_chunk(pieces, w_gate, w_up, w_down, keys=None):
    arrays, spans = [p[0] for p in pieces], [p[1] for p in pieces]
    total = sum(hi - lo for lo, hi in spans)
    width, hidden = w_gate.shape
    extra = [] if keys is None else [keys]
    rows = [2 * PAIR] * (total // (2 * PAIR))
    if extra:
        rows = [r + keys.shape[0] for r in rows]
    out = pl.pallas_call(
        functools.partial(expert_kernel, spans, bool(extra)),
        out_shape=[jax.ShapeDtypeStruct((r, width // 2), BF16) for r in rows]
        + [jax.ShapeDtypeStruct((total, hidden), BF16)] * 3,
        in_specs=vmem(len(extra) + len(pieces) + 3),
        out_specs=vmem(len(rows) + 3),
        name="expert",
        compiler_params=pltpu.CompilerParams(vmem_limit_bytes=20 << 20),
        cost_estimate=SHORT,
    )(*extra, *arrays, w_gate, w_up, w_down)
    return out[: len(rows)], out[len(rows) :]


def weight_kernel(spans, chunks, *refs):
    count = len(spans)
    payloads = refs[:count]
    small = refs[count : count + 3 * chunks]
    grad_gate, grad_up, grad_down = refs[count + 3 * chunks :]
    both = joined(payloads, spans)
    gate = jnp.concatenate([r[...] for r in small[0::3]], axis=0)
    up = jnp.concatenate([r[...] for r in small[1::3]], axis=0)
    hidden = jnp.concatenate([r[...] for r in small[2::3]], axis=0)
    grad_gate[...] = tn(both, gate).astype(BF16)
    grad_up[...] = tn(both, up).astype(BF16)
    grad_down[...] = tn(hidden, both).astype(BF16)


def weight_grads(pieces, small, width, hidden):
    count = len(pieces)
    payloads, spans = [p[0] for p in pieces], [p[1] for p in pieces]
    chunks = len(small)
    flat = [a for part in small for a in part]
    return pl.pallas_call(
        functools.partial(weight_kernel, spans, chunks),
        out_shape=[
            jax.ShapeDtypeStruct((width, hidden), BF16),
            jax.ShapeDtypeStruct((width, hidden), BF16),
            jax.ShapeDtypeStruct((hidden, width), BF16),
        ],
        in_specs=vmem(count + 3 * chunks),
        out_specs=vmem(3),
        name="weight_grads",
        compiler_params=pltpu.CompilerParams(vmem_limit_bytes=24 << 20),
        cost_estimate=SHORT,
    )(*payloads, *flat)


def combine_kernel(spans, ranks, grad_ref, *refs):
    returned, out = refs[:-1], refs[-1]
    rows = sum(hi - lo for lo, hi in spans)
    tokens = grad_ref.shape[0]
    block = returned[0][2 * PAIR : 2 * PAIR + ranks, :tokens].astype(F32)
    slot = returned[0][2 * PAIR : 2 * PAIR + ranks, tokens : 2 * tokens].astype(F32)
    keys = (PAIR * block + slot).astype(jnp.int32)
    half = grad_ref.shape[1] // 2
    own = jnp.zeros((rows, tokens), F32)
    for hit in match_rows(keys, 0, rows):
        own = jnp.where(hit, 1.0, own)
    first = is_first((rows, tokens))
    back = joined(returned, spans)
    for side in range(2):
        pick = jnp.where(first, own, 0.0) if side == 0 else jnp.where(first, 0.0, own)
        cols = slice(side * half, (side + 1) * half)
        total = grad_ref[:, cols].astype(F32) + tn(pick.astype(BF16), back)
        out[:, cols] = total.astype(BF16)


def combine(ranks, grads, pieces):
    returned, spans = [p[0] for p in pieces], [p[1] for p in pieces]
    return pl.pallas_call(
        functools.partial(combine_kernel, spans, ranks),
        out_shape=jax.ShapeDtypeStruct(grads.shape, BF16),
        in_specs=vmem(1 + len(returned)),
        out_specs=pl.BlockSpec(memory_space=pltpu.VMEM),
        name="combine",
        compiler_params=pltpu.CompilerParams(vmem_limit_bytes=16 << 20),
        cost_estimate=SHORT,
    )(grads, *returned)


def per_device(
    tokens_in,
    out_grad,
    route_weight,
    expert_ids,
    slot_pos,
    dropped,
    gate_weight,
    up_weight,
    down_weight,
):
    inputs = tokens_in[0]
    grads = out_grad[0]
    w_gate = gate_weight[0, 0]
    w_up = up_weight[0, 0]
    w_down = down_weight[0, 0]
    width, hidden = w_gate.shape
    n_expert = lax.axis_size("expert")
    n_pipe = lax.axis_size("pipe")
    me = lax.axis_index("expert")
    both_axes = ("pipe", "expert")

    def to_partner(value, k):
        return lax.ppermute(value, "expert", [(i, i ^ k) for i in range(n_expert)])

    def to_before(value, k):
        pairs = [
            (p * n_expert + i, (p - 1) * n_expert + (i ^ k))
            for p in range(1, n_pipe)
            for i in range(n_expert)
        ]
        return lax.ppermute(value, both_axes, pairs)

    live = (expert_ids[0] < n_expert) & (dropped[0] == 0)
    key = jnp.where(live, (expert_ids[0] ^ me) * PAIR + slot_pos[0], -1)
    keys = jnp.transpose(key)
    weight = jnp.transpose(route_weight[0])
    chips = n_expert // 2
    near = list(range(1, chips // 2))
    early = list(range(chips // 2, 3 * chips // 4))
    late = list(range(3 * chips // 4, chips))
    sent = gather(keys, weight, inputs, grads, chips, [0] + late)
    mine = (0, PAIR)

    def after(values, event):
        return lax.optimization_barrier((values, event))[0]

    def forward(value, *cuts):
        edges = [PAIR, *cuts, 2 * PAIR]
        pieces = [(value, mine)]
        for lo, hi in zip(edges, edges[1:]):
            pieces.append((to_partner(value[lo:hi], 1), (0, hi - lo)))
        return pieces

    def gated(pieces, event):
        values = after([p[0] for p in pieces], event)
        return [(v, p[1]) for v, p in zip(values, pieces)]

    arrived, order, small, returned = {}, [], [], {}

    def process(chunk, pieces, **options):
        back, parts = expert_chunk(pieces, w_gate, w_up, w_down, **options)
        order.extend(pieces)
        small.append(parts)
        for c, value in zip(chunk, back):
            returned[c] = to_before(value, 2 * c)
        return parts

    for c in early + near:
        arrived[c] = to_partner(sent[c], 2 * c)
    for c in late:
        arrived[c] = [(to_partner(v, 2 * c + i), mine) for i, v in enumerate(sent[c])]
    beside = to_partner(sent[0][1], 1)
    next_grads = to_before(after(grads, sent[0][0]), 0)
    pieces = [(sent[0][0], mine), (beside, mine)]
    for c in near:
        pieces += forward(arrived[c])
    parts = process([0] + near, pieces, keys=keys)
    pieces = [piece for c in early for piece in forward(arrived[c], PAIR + 24)]
    parts = process(early, gated(pieces, parts))
    pieces = [piece for c in late for piece in arrived[c]]
    process(late, gated(pieces, (parts, next_grads)))
    small[0] = after(small[0], [returned[c] for c in [0] + near])
    grad_gate, grad_up, grad_down = weight_grads(order, small, width, hidden)
    pieces = []
    for c in range(chips):
        value = after(returned[c], grad_gate) if c not in late else returned[c]
        pieces += forward(value)
    upstream = combine(keys.shape[0], next_grads, pieces)
    return (upstream[None], grad_gate[None, None], grad_up[None, None], grad_down[None, None])


def solution(mesh):
    return jax.shard_map(
        per_device,
        mesh=mesh,
        in_specs=(
            P("pipe", "expert", None),
            P("pipe", "expert", None),
            P("pipe", "expert", None),
            P("pipe", "expert", None),
            P("pipe", "expert", None),
            P("pipe", "expert", None),
            P("pipe", "expert", None, None),
            P("pipe", "expert", None, None),
            P("pipe", "expert", None, None),
        ),
        out_specs=(
            P("pipe", "expert", None),
            P("pipe", "expert", None, None),
            P("pipe", "expert", None, None),
            P("pipe", "expert", None, None),
        ),
        check_vma=False,
    )
```

```python
import functools

import jax
import jax.numpy as jnp
from jax import lax
from jax.experimental import pallas as pl
from jax.experimental.pallas import tpu as pltpu
from jax.sharding import PartitionSpec as P

CAP = 20
PAIR = 2 * CAP
F32 = jnp.float32
BF16 = jnp.bfloat16
SHORT = pl.CostEstimate(flops=1, transcendentals=0, bytes_accessed=1)


def vmem(count):
    return [pl.BlockSpec(memory_space=pltpu.VMEM)] * count


def is_first(shape):
    return lax.rem(lax.broadcasted_iota(jnp.int32, shape, 0), PAIR) < CAP


def match_rows(keys, first_row, rows):
    tokens = keys.shape[1]
    row = lax.broadcasted_iota(jnp.int32, (rows, tokens), 0)
    slot = first_row + row - jnp.where(lax.rem(row, PAIR) < CAP, 0, CAP)
    return [keys[k : k + 1, :] == slot for k in range(keys.shape[0])]


def gather_kernel(n_expert, ids_hbm, slot_hbm, dropped_hbm, weight_hbm, in_hbm, grad_hbm, keys_ref, *refs):
    outs, (ids_ref, slot_ref, dropped_ref, weight_ref, in_ref, grad_ref, sem) = refs[:-7], refs[-7:]
    copies = [
        pltpu.make_async_copy(src, dst, sem.at[i])
        for i, (src, dst) in enumerate(
            (
                (ids_hbm, ids_ref),
                (slot_hbm, slot_ref),
                (dropped_hbm, dropped_ref),
                (weight_hbm, weight_ref),
                (in_hbm, in_ref),
                (grad_hbm, grad_ref),
            )
        )
    ]
    for copy in copies:
        copy.start()
    me = lax.axis_index("expert")
    for copy in copies[:4]:
        copy.wait()
    ids = ids_ref[...]
    live = (ids < n_expert) & (dropped_ref[...] == 0)
    keys = jnp.where(live, (ids ^ me) * PAIR + slot_ref[...], -1)
    keys_ref[...] = keys
    weight = weight_ref[...]
    rows = sum(out.shape[0] for out in outs)
    tokens = keys.shape[1]
    own = jnp.zeros((rows, tokens), F32)
    scaled = jnp.zeros((rows, tokens), F32)
    for k, hit in enumerate(match_rows(keys, 0, rows)):
        own = jnp.where(hit, 1.0, own)
        scaled = jnp.where(hit, weight[k : k + 1, :], scaled)
    first = is_first((rows, tokens))
    pick_in = jnp.where(first, own, 0.0).astype(BF16)
    pick_grad = jnp.where(first, 0.0, own).astype(BF16)
    row_weight = jnp.sum(scaled, axis=1, keepdims=True)
    copies[4].wait()
    got = jnp.dot(pick_in, in_ref[...], preferred_element_type=F32)
    copies[5].wait()
    got = got + row_weight * jnp.dot(pick_grad, grad_ref[...], preferred_element_type=F32)
    got = got.astype(BF16)
    start = 0
    for out in outs:
        out[...] = got[start : start + out.shape[0], :]
        start += out.shape[0]


def gather(ids, slots, dropped, weight, inputs, grads, chips, apart):
    tokens, width = inputs.shape
    ranks = ids.shape[0]
    sizes = [n for c in range(chips) for n in ([PAIR, PAIR] if c in apart else [2 * PAIR])]
    outs = pl.pallas_call(
        functools.partial(gather_kernel, 2 * chips),
        out_shape=[jax.ShapeDtypeStruct((ranks, tokens), jnp.int32)]
        + [jax.ShapeDtypeStruct((n, width), BF16) for n in sizes],
        in_specs=[pl.BlockSpec(memory_space=pltpu.HBM)] * 6,
        out_specs=vmem(1 + len(sizes)),
        scratch_shapes=[pltpu.VMEM((ranks, tokens), jnp.int32)] * 3
        + [pltpu.VMEM((ranks, tokens), F32)]
        + [pltpu.VMEM((tokens, width), BF16)] * 2
        + [pltpu.SemaphoreType.DMA((6,))],
        name="gather",
        compiler_params=pltpu.CompilerParams(vmem_limit_bytes=16 << 20),
        cost_estimate=SHORT,
    )(*(pltpu.with_memory_space_constraint(a, pltpu.HBM) for a in (ids, slots, dropped, weight, inputs, grads)))
    keys, *outs = outs
    return keys, [[outs.pop(0), outs.pop(0)] if c in apart else outs.pop(0) for c in range(chips)]


def load_kernel(count, *refs):
    sem = refs[-1]
    copies = [pltpu.make_async_copy(refs[i], refs[count + i], sem.at[i]) for i in range(count)]
    for copy in copies:
        copy.start()
    for copy in copies:
        copy.wait()


def load(*arrays):
    return pl.pallas_call(
        functools.partial(load_kernel, len(arrays)),
        out_shape=[jax.ShapeDtypeStruct(a.shape, a.dtype) for a in arrays],
        in_specs=[pl.BlockSpec(memory_space=pltpu.HBM)] * len(arrays),
        out_specs=vmem(len(arrays)),
        scratch_shapes=[pltpu.SemaphoreType.DMA((len(arrays),))],
        name="load",
        compiler_params=pltpu.CompilerParams(vmem_limit_bytes=12 << 20),
        cost_estimate=SHORT,
    )(*arrays)


def nt(a, b):
    return lax.dot_general(a, b, (((1,), (1,)), ((), ())), preferred_element_type=F32)


def tn(a, b):
    return lax.dot_general(a, b, (((0,), (0,)), ((), ())), preferred_element_type=F32)


def joined(refs, spans):
    return jnp.concatenate([r[lo:hi, :] for r, (lo, hi) in zip(refs, spans)], axis=0)


def expert_kernel(spans, with_keys, *refs):
    count = len(spans)
    if with_keys:
        keys_ref, refs = refs[0], refs[1:]
    payloads = refs[:count]
    w_gate, w_up, w_down = refs[count : count + 3]
    returns = refs[count + 3 : -3]
    gate_out, up_out, hidden_out = refs[-3:]
    rows = sum(hi - lo for lo, hi in spans)
    half = w_gate.shape[0] // 2
    both = joined(payloads, spans)
    gate_pre = jnp.dot(both, w_gate[...], preferred_element_type=F32)
    up_pre = jnp.dot(both, w_up[...], preferred_element_type=F32)
    hidden_grad = pltpu.roll(nt(both, w_down[...]), rows - CAP, 0)
    first = is_first(gate_pre.shape)
    sigma = jax.nn.sigmoid(gate_pre)
    active = gate_pre * sigma
    hidden = jnp.where(first, active * up_pre, 0.0)
    gate_grad = hidden_grad * up_pre * sigma * (1.0 + gate_pre * (1.0 - sigma))
    gate_grad = jnp.where(first, gate_grad, 0.0)
    up_grad = jnp.where(first, hidden_grad * active, 0.0)
    gate_out[...] = gate_grad.astype(BF16)
    up_out[...] = up_grad.astype(BF16)
    hidden_out[...] = pltpu.roll(hidden, CAP, 0).astype(BF16)
    gate_two = (gate_grad + pltpu.roll(gate_grad, CAP, 0)).astype(BF16)
    up_two = (up_grad + pltpu.roll(up_grad, CAP, 0)).astype(BF16)
    left = nt(gate_two, w_gate[:half, :]) + nt(up_two, w_up[:half, :])
    right = nt(gate_two, w_gate[half:, :]) + nt(up_two, w_up[half:, :])
    row_grad = jnp.where(is_first(left.shape), left, right).astype(BF16)
    step = rows // len(returns)
    for k, out in enumerate(returns):
        out[:step, :] = row_grad[k * step : (k + 1) * step, :]
    if with_keys:
        ranks, tokens = keys_ref.shape
        keys = keys_ref[...].astype(F32)
        block = jnp.floor((keys + 0.5) / PAIR)
        for out in returns:
            out[2 * PAIR :, :tokens] = block.astype(BF16)
            out[2 * PAIR :, tokens : 2 * tokens] = (keys - PAIR * block).astype(BF16)
            out[2 * PAIR :, 2 * tokens :] = jnp.zeros((ranks, half - 2 * tokens), BF16)


def expert_chunk(pieces, w_gate, w_up, w_down, keys=None):
    arrays, spans = [p[0] for p in pieces], [p[1] for p in pieces]
    total = sum(hi - lo for lo, hi in spans)
    width, hidden = w_gate.shape
    extra = [] if keys is None else [keys]
    rows = [2 * PAIR] * (total // (2 * PAIR))
    if extra:
        rows = [r + keys.shape[0] for r in rows]
    out = pl.pallas_call(
        functools.partial(expert_kernel, spans, bool(extra)),
        out_shape=[jax.ShapeDtypeStruct((r, width // 2), BF16) for r in rows]
        + [jax.ShapeDtypeStruct((total, hidden), BF16)] * 3,
        in_specs=vmem(len(extra) + len(pieces) + 3),
        out_specs=vmem(len(rows) + 3),
        name="expert",
        compiler_params=pltpu.CompilerParams(vmem_limit_bytes=20 << 20),
        cost_estimate=SHORT,
    )(*extra, *arrays, w_gate, w_up, w_down)
    return out[: len(rows)], out[len(rows) :]


def weight_kernel(spans, chunks, *refs):
    count = len(spans)
    payloads = refs[:count]
    small = refs[count : count + 3 * chunks]
    grad_gate, grad_up, grad_down = refs[count + 3 * chunks :]
    both = joined(payloads, spans)
    gate = jnp.concatenate([r[...] for r in small[0::3]], axis=0)
    up = jnp.concatenate([r[...] for r in small[1::3]], axis=0)
    hidden = jnp.concatenate([r[...] for r in small[2::3]], axis=0)
    grad_gate[...] = tn(both, gate).astype(BF16)
    grad_up[...] = tn(both, up).astype(BF16)
    grad_down[...] = tn(hidden, both).astype(BF16)


def weight_grads(pieces, small, width, hidden):
    count = len(pieces)
    payloads, spans = [p[0] for p in pieces], [p[1] for p in pieces]
    chunks = len(small)
    flat = [a for part in small for a in part]
    return pl.pallas_call(
        functools.partial(weight_kernel, spans, chunks),
        out_shape=[
            jax.ShapeDtypeStruct((width, hidden), BF16),
            jax.ShapeDtypeStruct((width, hidden), BF16),
            jax.ShapeDtypeStruct((hidden, width), BF16),
        ],
        in_specs=vmem(count + 3 * chunks),
        out_specs=vmem(3),
        name="weight_grads",
        compiler_params=pltpu.CompilerParams(vmem_limit_bytes=24 << 20),
        cost_estimate=SHORT,
    )(*payloads, *flat)


def combine_kernel(spans, ranks, grad_ref, *refs):
    returned, out = refs[:-1], refs[-1]
    rows = sum(hi - lo for lo, hi in spans)
    tokens = grad_ref.shape[0]
    block = returned[0][2 * PAIR : 2 * PAIR + ranks, :tokens].astype(F32)
    slot = returned[0][2 * PAIR : 2 * PAIR + ranks, tokens : 2 * tokens].astype(F32)
    keys = (PAIR * block + slot).astype(jnp.int32)
    half = grad_ref.shape[1] // 2
    own = jnp.zeros((rows, tokens), F32)
    for hit in match_rows(keys, 0, rows):
        own = jnp.where(hit, 1.0, own)
    first = is_first((rows, tokens))
    back = joined(returned, spans)
    for side in range(2):
        pick = jnp.where(first, own, 0.0) if side == 0 else jnp.where(first, 0.0, own)
        cols = slice(side * half, (side + 1) * half)
        total = grad_ref[:, cols].astype(F32) + tn(pick.astype(BF16), back)
        out[:, cols] = total.astype(BF16)


def combine(ranks, grads, pieces):
    returned, spans = [p[0] for p in pieces], [p[1] for p in pieces]
    return pl.pallas_call(
        functools.partial(combine_kernel, spans, ranks),
        out_shape=jax.ShapeDtypeStruct(grads.shape, BF16),
        in_specs=vmem(1 + len(returned)),
        out_specs=pl.BlockSpec(memory_space=pltpu.VMEM),
        name="combine",
        compiler_params=pltpu.CompilerParams(vmem_limit_bytes=16 << 20),
        cost_estimate=SHORT,
    )(grads, *returned)


def per_device(
    tokens_in,
    out_grad,
    route_weight,
    expert_ids,
    slot_pos,
    dropped,
    gate_weight,
    up_weight,
    down_weight,
):
    inputs = tokens_in[0]
    grads = out_grad[0]
    w_gate = gate_weight[0, 0]
    w_up = up_weight[0, 0]
    w_down = down_weight[0, 0]
    width, hidden = w_gate.shape
    n_expert = lax.axis_size("expert")
    n_pipe = lax.axis_size("pipe")
    both_axes = ("pipe", "expert")

    def to_partner(value, k):
        return lax.ppermute(value, "expert", [(i, i ^ k) for i in range(n_expert)])

    def to_before(value, k):
        pairs = [
            (p * n_expert + i, (p - 1) * n_expert + (i ^ k))
            for p in range(1, n_pipe)
            for i in range(n_expert)
        ]
        return lax.ppermute(value, both_axes, pairs)

    chips = n_expert // 2
    near = list(range(1, chips // 2))
    early = list(range(chips // 2, 3 * chips // 4))
    late = list(range(3 * chips // 4, chips))
    by_rank = [jnp.transpose(a[0]) for a in (expert_ids, slot_pos, dropped, route_weight)]
    keys, sent = gather(*by_rank, inputs, grads, chips, [0] + late)
    mine = (0, PAIR)

    def after(values, event):
        return lax.optimization_barrier((values, event))[0]

    def forward(value, *cuts):
        edges = [PAIR, *cuts, 2 * PAIR]
        pieces = [(value, mine)]
        for lo, hi in zip(edges, edges[1:]):
            pieces.append((to_partner(value[lo:hi], 1), (0, hi - lo)))
        return pieces

    def gated(pieces, event):
        values = after([p[0] for p in pieces], event)
        return [(v, p[1]) for v, p in zip(values, pieces)]

    arrived, order, small, returned = {}, [], [], {}

    def process(chunk, pieces, **options):
        back, parts = expert_chunk(pieces, w_gate, w_up, w_down, **options)
        order.extend(pieces)
        small.append(parts)
        for c, value in zip(chunk, back):
            returned[c] = to_before(value, 2 * c)
        return parts

    for c in early + near:
        arrived[c] = to_partner(sent[c], 2 * c)
    for c in late:
        arrived[c] = [(to_partner(v, 2 * c + i), mine) for i, v in enumerate(sent[c])]
    beside = to_partner(sent[0][1], 1)
    next_grads = to_before(after(grads, sent[0][0]), 0)
    pieces = [(sent[0][0], mine), (beside, mine)]
    w_gate, w_up, w_down = load(*after((w_gate, w_up, w_down), sent[0][0]))
    here = after([arrived[c] for c in near], w_down)
    for value in here:
        pieces += forward(value)
    parts = process([0] + near, pieces, keys=keys)
    pieces = [piece for c in early for piece in forward(arrived[c], PAIR + 24)]
    parts = process(early, gated(pieces, parts))
    pieces = [piece for c in late for piece in arrived[c]]
    process(late, gated(pieces, (parts, next_grads)))
    small[0] = after(small[0], [returned[c] for c in [0] + near])
    grad_gate, grad_up, grad_down = weight_grads(order, small, width, hidden)
    pieces = []
    for c in range(chips):
        value = after(returned[c], grad_gate) if c not in late else returned[c]
        pieces += forward(value)
    upstream = combine(keys.shape[0], next_grads, pieces)
    return (upstream[None], grad_gate[None, None], grad_up[None, None], grad_down[None, None])


def solution(mesh):
    return jax.shard_map(
        per_device,
        mesh=mesh,
        in_specs=(
            P("pipe", "expert", None),
            P("pipe", "expert", None),
            P("pipe", "expert", None),
            P("pipe", "expert", None),
            P("pipe", "expert", None),
            P("pipe", "expert", None),
            P("pipe", "expert", None, None),
            P("pipe", "expert", None, None),
            P("pipe", "expert", None, None),
        ),
        out_specs=(
            P("pipe", "expert", None),
            P("pipe", "expert", None, None),
            P("pipe", "expert", None, None),
            P("pipe", "expert", None, None),
        ),
        check_vma=False,
    )
```

```python
import functools

import jax
import jax.numpy as jnp
from jax import lax
from jax.experimental import pallas as pl
from jax.experimental.pallas import tpu as pltpu
from jax.sharding import PartitionSpec as P

CAP = 20
PAIR = 2 * CAP
SHARES = 2
F32 = jnp.float32
BF16 = jnp.bfloat16
SHORT = pl.CostEstimate(flops=1, transcendentals=0, bytes_accessed=1)


def vmem(count):
    return [pl.BlockSpec(memory_space=pltpu.VMEM)] * count


def is_first(shape):
    return lax.rem(lax.broadcasted_iota(jnp.int32, shape, 0), PAIR) < CAP


def match_rows(keys, first_row, rows):
    tokens = keys.shape[1]
    row = lax.broadcasted_iota(jnp.int32, (rows, tokens), 0)
    slot = first_row + row - jnp.where(lax.rem(row, PAIR) < CAP, 0, CAP)
    return [keys[k : k + 1, :] == slot for k in range(keys.shape[0])]


def gather_kernel(n_expert, shares, ids_hbm, slot_hbm, dropped_hbm, weight_hbm, in_hbm, grad_hbm, keys_ref, *refs):
    grad_refs, outs = refs[:shares], refs[shares:-6]
    ids_ref, slot_ref, dropped_ref, weight_ref, in_ref, sem = refs[-6:]
    share = grad_refs[0].shape[0]
    copies = [
        pltpu.make_async_copy(src, dst, sem.at[i])
        for i, (src, dst) in enumerate(
            (
                (ids_hbm, ids_ref),
                (slot_hbm, slot_ref),
                (dropped_hbm, dropped_ref),
                (weight_hbm, weight_ref),
                (in_hbm, in_ref),
                *((grad_hbm.at[pl.ds(i * share, share)], ref) for i, ref in enumerate(grad_refs)),
            )
        )
    ]
    for copy in copies:
        copy.start()
    me = lax.axis_index("expert")
    for copy in copies[:4]:
        copy.wait()
    ids = ids_ref[...]
    live = (ids < n_expert) & (dropped_ref[...] == 0)
    keys = jnp.where(live, (ids ^ me) * PAIR + slot_ref[...], -1)
    keys_ref[...] = keys
    weight = weight_ref[...]
    rows = sum(out.shape[0] for out in outs)
    tokens = keys.shape[1]
    own = jnp.zeros((rows, tokens), F32)
    scaled = jnp.zeros((rows, tokens), F32)
    for k, hit in enumerate(match_rows(keys, 0, rows)):
        own = jnp.where(hit, 1.0, own)
        scaled = jnp.where(hit, weight[k : k + 1, :], scaled)
    first = is_first((rows, tokens))
    pick_in = jnp.where(first, own, 0.0).astype(BF16)
    pick_grad = jnp.where(first, 0.0, own).astype(BF16)
    row_weight = jnp.sum(scaled, axis=1, keepdims=True)
    copies[4].wait()
    got = jnp.dot(pick_in, in_ref[...], preferred_element_type=F32)
    for i, ref in enumerate(grad_refs):
        copies[5 + i].wait()
        pick = pick_grad[:, i * share : (i + 1) * share]
        got = got + row_weight * jnp.dot(pick, ref[...], preferred_element_type=F32)
    got = got.astype(BF16)
    start = 0
    for out in outs:
        out[...] = got[start : start + out.shape[0], :]
        start += out.shape[0]


def gather(ids, slots, dropped, weight, inputs, grads, chips, apart, shares):
    tokens, width = inputs.shape
    ranks = ids.shape[0]
    sizes = [n for c in range(chips) for n in ([PAIR, PAIR] if c in apart else [2 * PAIR])]
    outs = pl.pallas_call(
        functools.partial(gather_kernel, 2 * chips, shares),
        out_shape=[jax.ShapeDtypeStruct((ranks, tokens), jnp.int32)]
        + [jax.ShapeDtypeStruct((tokens // shares, width), BF16)] * shares
        + [jax.ShapeDtypeStruct((n, width), BF16) for n in sizes],
        in_specs=[pl.BlockSpec(memory_space=pltpu.HBM)] * 6,
        out_specs=vmem(1 + shares + len(sizes)),
        scratch_shapes=[pltpu.VMEM((ranks, tokens), jnp.int32)] * 3
        + [pltpu.VMEM((ranks, tokens), F32)]
        + [pltpu.VMEM((tokens, width), BF16)]
        + [pltpu.SemaphoreType.DMA((5 + shares,))],
        name="gather",
        compiler_params=pltpu.CompilerParams(vmem_limit_bytes=16 << 20),
        cost_estimate=SHORT,
    )(*pinned((ids, slots, dropped, weight, inputs, grads)))
    keys, held, outs = outs[0], outs[1 : 1 + shares], list(outs[1 + shares :])
    return keys, held, [[outs.pop(0), outs.pop(0)] if c in apart else outs.pop(0) for c in range(chips)]


def load_kernel(gate_hbm, up_hbm, down_hbm, both_ref, down_ref, sem):
    hidden = gate_hbm.shape[1]
    copies = [
        pltpu.make_async_copy(gate_hbm, both_ref.at[:, :hidden], sem.at[0]),
        pltpu.make_async_copy(up_hbm, both_ref.at[:, hidden:], sem.at[1]),
        pltpu.make_async_copy(down_hbm, down_ref, sem.at[2]),
    ]
    for copy in copies:
        copy.start()
    for copy in copies:
        copy.wait()


def pinned(arrays):
    return [pltpu.with_memory_space_constraint(a, pltpu.HBM) for a in arrays]


def load(w_gate, w_up, w_down):
    width, hidden = w_gate.shape
    return pl.pallas_call(
        load_kernel,
        out_shape=[
            jax.ShapeDtypeStruct((width, 2 * hidden), BF16),
            jax.ShapeDtypeStruct((hidden, width), BF16),
        ],
        in_specs=[pl.BlockSpec(memory_space=pltpu.HBM)] * 3,
        out_specs=vmem(2),
        scratch_shapes=[pltpu.SemaphoreType.DMA((3,))],
        name="load",
        compiler_params=pltpu.CompilerParams(vmem_limit_bytes=12 << 20),
        cost_estimate=SHORT,
    )(*pinned((w_gate, w_up, w_down)))


def nt(a, b):
    return lax.dot_general(a, b, (((1,), (1,)), ((), ())), preferred_element_type=F32)


def tn(a, b):
    return lax.dot_general(a, b, (((0,), (0,)), ((), ())), preferred_element_type=F32)


def joined(refs, spans):
    return jnp.concatenate([r[lo:hi, :] for r, (lo, hi) in zip(refs, spans)], axis=0)


def expert_kernel(spans, with_keys, *refs):
    count = len(spans)
    if with_keys:
        keys_ref, refs = refs[0], refs[1:]
    payloads = refs[:count]
    w_both, w_down = refs[count : count + 2]
    returns = refs[count + 2 : -2]
    grads_out, hidden_out = refs[-2:]
    rows = sum(hi - lo for lo, hi in spans)
    width, units = w_down.shape[1], w_down.shape[0]
    half = width // 2
    both = joined(payloads, spans)
    pre = jnp.dot(both, w_both[...], preferred_element_type=F32)
    gate_pre, up_pre = pre[:, :units], pre[:, units:]
    hidden_grad = pltpu.roll(nt(both, w_down[...]), rows - CAP, 0)
    first = is_first(gate_pre.shape)
    sigma = jax.nn.sigmoid(gate_pre)
    active = gate_pre * sigma
    hidden = jnp.where(first, active * up_pre, 0.0)
    gate_grad = hidden_grad * up_pre * sigma * (1.0 + gate_pre * (1.0 - sigma))
    gate_grad = jnp.where(first, gate_grad, 0.0)
    up_grad = jnp.where(first, hidden_grad * active, 0.0)
    grads = jnp.concatenate([gate_grad, up_grad], axis=1)
    grads_two = (grads + pltpu.roll(grads, CAP, 0)).astype(BF16)
    left = nt(grads_two, w_both[:half, :])
    right = nt(grads_two, w_both[half:, :])
    row_grad = jnp.where(is_first(left.shape), left, right).astype(BF16)
    step = rows // len(returns)
    for k, out in enumerate(returns):
        out[:step, :] = row_grad[k * step : (k + 1) * step, :]
    grads_out[...] = grads.astype(BF16)
    hidden_out[...] = pltpu.roll(hidden, CAP, 0).astype(BF16)
    if with_keys:
        ranks, tokens = keys_ref.shape
        keys = keys_ref[...].astype(F32)
        block = jnp.floor((keys + 0.5) / PAIR)
        for out in returns:
            out[2 * PAIR :, :tokens] = block.astype(BF16)
            out[2 * PAIR :, tokens : 2 * tokens] = (keys - PAIR * block).astype(BF16)
            out[2 * PAIR :, 2 * tokens :] = jnp.zeros((ranks, half - 2 * tokens), BF16)


def expert_chunk(pieces, w_both, w_down, keys=None):
    arrays, spans = [p[0] for p in pieces], [p[1] for p in pieces]
    total = sum(hi - lo for lo, hi in spans)
    hidden, width = w_down.shape
    extra = [] if keys is None else [keys]
    rows = [2 * PAIR] * (total // (2 * PAIR))
    if extra:
        rows = [r + keys.shape[0] for r in rows]
    out = pl.pallas_call(
        functools.partial(expert_kernel, spans, bool(extra)),
        out_shape=[jax.ShapeDtypeStruct((r, width // 2), BF16) for r in rows]
        + [jax.ShapeDtypeStruct((total, n * hidden), BF16) for n in (2, 1)],
        in_specs=vmem(len(extra) + len(pieces) + 2),
        out_specs=vmem(len(rows) + 2),
        name="expert",
        compiler_params=pltpu.CompilerParams(vmem_limit_bytes=20 << 20),
        cost_estimate=SHORT,
    )(*extra, *arrays, w_both, w_down)
    return out[: len(rows)], out[len(rows) :]


def weight_kernel(spans, chunks, *refs):
    count = len(spans)
    payloads = refs[:count]
    small = refs[count : count + 2 * chunks]
    grad_gate, grad_up, grad_down = refs[count + 2 * chunks :]
    units = grad_gate.shape[1]
    both = joined(payloads, spans)
    grads = jnp.concatenate([r[...] for r in small[0::2]], axis=0)
    hidden = jnp.concatenate([r[...] for r in small[1::2]], axis=0)
    made = tn(both, grads).astype(BF16)
    grad_gate[...] = made[:, :units]
    grad_up[...] = made[:, units:]
    grad_down[...] = tn(hidden, both).astype(BF16)


def weight_grads(pieces, small, width, hidden):
    count = len(pieces)
    payloads, spans = [p[0] for p in pieces], [p[1] for p in pieces]
    chunks = len(small)
    flat = [a for part in small for a in part]
    return pl.pallas_call(
        functools.partial(weight_kernel, spans, chunks),
        out_shape=[
            jax.ShapeDtypeStruct((width, hidden), BF16),
            jax.ShapeDtypeStruct((width, hidden), BF16),
            jax.ShapeDtypeStruct((hidden, width), BF16),
        ],
        in_specs=vmem(count + 2 * chunks),
        out_specs=vmem(3),
        name="weight_grads",
        compiler_params=pltpu.CompilerParams(vmem_limit_bytes=24 << 20),
        cost_estimate=SHORT,
    )(*payloads, *flat)


def combine_kernel(spans, start, ranks, bases, keys_ref, *refs):
    base_refs, returned = refs[:bases], refs[bases : bases + len(spans)]
    out, *scratch = refs[bases + len(spans) :]
    rows = sum(hi - lo for lo, hi in spans)
    share = base_refs[0].shape[0]
    tokens, width = out.shape
    block = keys_ref[2 * PAIR : 2 * PAIR + ranks, :tokens].astype(F32)
    slot = keys_ref[2 * PAIR : 2 * PAIR + ranks, tokens : 2 * tokens].astype(F32)
    keys = (PAIR * block + slot).astype(jnp.int32)
    own = jnp.zeros((rows, tokens), F32)
    for hit in match_rows(keys, start * PAIR, rows):
        own = jnp.where(hit, 1.0, own)
    first = is_first((rows, tokens))
    picks = [jnp.where(first, own, 0.0).astype(BF16), jnp.where(first, 0.0, own).astype(BF16)]
    back = joined(returned, spans)
    quarter = width // 4
    copies = []
    for i in range(4):
        cols = slice(i * quarter, (i + 1) * quarter)
        side = slice(i % 2 * quarter, (i % 2 + 1) * quarter)
        added = tn(picks[i // 2], back[:, side])
        for j, ref in enumerate(base_refs):
            here = slice(j * share, (j + 1) * share)
            total = ref[:, cols].astype(F32) + added[here, :]
            (scratch[0] if scratch else out)[here, cols] = total.astype(out.dtype)
        if scratch:
            copy = pltpu.make_async_copy(scratch[0].at[:, cols], out.at[:, cols], scratch[1].at[i])
            copy.start()
            copies.append(copy)
    for copy in copies:
        copy.wait()


def combine(ranks, carrier, bases, start, pieces, last):
    returned, spans = [p[0] for p in pieces], [p[1] for p in pieces]
    shape = (len(bases) * bases[0].shape[0], bases[0].shape[1])
    space = pltpu.HBM if last else pltpu.VMEM
    return pl.pallas_call(
        functools.partial(combine_kernel, spans, start, ranks, len(bases)),
        out_shape=jax.ShapeDtypeStruct(shape, BF16 if last else F32),
        in_specs=vmem(1 + len(bases) + len(returned)),
        out_specs=pl.BlockSpec(memory_space=space),
        scratch_shapes=[pltpu.VMEM(shape, BF16), pltpu.SemaphoreType.DMA((4,))] if last else [],
        name="combine",
        compiler_params=pltpu.CompilerParams(vmem_limit_bytes=16 << 20),
        cost_estimate=SHORT,
    )(carrier, *bases, *returned)


def per_device(
    tokens_in,
    out_grad,
    route_weight,
    expert_ids,
    slot_pos,
    dropped,
    gate_weight,
    up_weight,
    down_weight,
):
    inputs = tokens_in[0]
    grads = out_grad[0]
    w_gate = gate_weight[0, 0]
    w_up = up_weight[0, 0]
    w_down = down_weight[0, 0]
    width, hidden = w_gate.shape
    n_expert = lax.axis_size("expert")
    n_pipe = lax.axis_size("pipe")
    both_axes = ("pipe", "expert")

    def to_partner(value, k):
        return lax.ppermute(value, "expert", [(i, i ^ k) for i in range(n_expert)])

    def to_before(value, k):
        pairs = [
            (p * n_expert + i, (p - 1) * n_expert + (i ^ k))
            for p in range(1, n_pipe)
            for i in range(n_expert)
        ]
        return lax.ppermute(value, both_axes, pairs)

    chips = n_expert // 2
    near = list(range(1, chips // 2))
    early = list(range(chips // 2, 3 * chips // 4))
    late = list(range(3 * chips // 4, chips))
    by_rank = [jnp.transpose(a[0]) for a in (expert_ids, slot_pos, dropped, route_weight)]
    keys, held, sent = gather(*by_rank, inputs, grads, chips, [0] + late, SHARES)
    mine = (0, PAIR)

    def after(values, event):
        return lax.optimization_barrier((values, event))[0]

    def forward(value, *cuts):
        edges = [PAIR, *cuts, 2 * PAIR]
        pieces = [(value, mine)]
        for lo, hi in zip(edges, edges[1:]):
            pieces.append((to_partner(value[lo:hi], 1), (0, hi - lo)))
        return pieces

    def gated(pieces, event):
        values = after([p[0] for p in pieces], event)
        return [(v, p[1]) for v, p in zip(values, pieces)]

    arrived, order, small, returned = {}, [], [], {}

    def process(chunk, pieces, **options):
        back, parts = expert_chunk(pieces, w_both, w_down, **options)
        order.extend(pieces)
        small.append(parts)
        for c, value in zip(chunk, back):
            returned[c] = to_before(value, 2 * c)
        return parts

    for c in early + near:
        arrived[c] = to_partner(sent[c], 2 * c)
    for c in late:
        arrived[c] = [(to_partner(v, 2 * c + i), mine) for i, v in enumerate(sent[c])]
    beside = to_partner(sent[0][1], 1)
    next_grads = [to_before(share, 0) for share in held]
    pieces = [(sent[0][0], mine), (beside, mine)]
    w_both, w_down = load(*after((w_gate, w_up, w_down), sent[0][0]))
    here = after([arrived[c] for c in near], w_down)
    for value in here:
        pieces += forward(value)
    parts = process([0] + near, pieces, keys=keys)
    pieces = [piece for c in early for piece in forward(arrived[c], PAIR + 24)]
    parts = process(early, gated(pieces, (parts, next_grads[0])))
    pieces = [piece for c in late for piece in arrived[c]]
    process(late, gated(pieces, (parts, next_grads)))
    small[0] = after(small[0], [returned[c] for c in [0] + near])
    grad_gate, grad_up, grad_down = weight_grads(order, small, width, hidden)
    carrier = returned[0]
    pieces = []
    for c in range(chips):
        value = after(returned[c], grad_gate) if c not in late else returned[c]
        pieces += forward(value)
    upstream = combine(keys.shape[0], carrier, next_grads, 0, pieces, True)
    return (upstream[None], grad_gate[None, None], grad_up[None, None], grad_down[None, None])


def solution(mesh):
    return jax.shard_map(
        per_device,
        mesh=mesh,
        in_specs=(
            P("pipe", "expert", None),
            P("pipe", "expert", None),
            P("pipe", "expert", None),
            P("pipe", "expert", None),
            P("pipe", "expert", None),
            P("pipe", "expert", None),
            P("pipe", "expert", None, None),
            P("pipe", "expert", None, None),
            P("pipe", "expert", None, None),
        ),
        out_specs=(
            P("pipe", "expert", None),
            P("pipe", "expert", None, None),
            P("pipe", "expert", None, None),
            P("pipe", "expert", None, None),
        ),
        check_vma=False,
    )
```

```python
import functools

import jax
import jax.numpy as jnp
from jax import lax
from jax.experimental import pallas as pl
from jax.experimental.pallas import tpu as pltpu
from jax.sharding import PartitionSpec as P

CAP = 20
PAIR = 2 * CAP
SHARES = 2
F32 = jnp.float32
BF16 = jnp.bfloat16
SHORT = pl.CostEstimate(flops=1, transcendentals=0, bytes_accessed=1)


def vmem(count):
    return [pl.BlockSpec(memory_space=pltpu.VMEM)] * count


def is_first(shape):
    return lax.rem(lax.broadcasted_iota(jnp.int32, shape, 0), PAIR) < CAP


def match_rows(keys, first_row, rows):
    tokens = keys.shape[1]
    row = lax.broadcasted_iota(jnp.int32, (rows, tokens), 0)
    slot = first_row + row - jnp.where(lax.rem(row, PAIR) < CAP, 0, CAP)
    return [keys[k : k + 1, :] == slot for k in range(keys.shape[0])]


def gather_kernel(n_expert, shares, ids_hbm, slot_hbm, dropped_hbm, weight_hbm, in_hbm, grad_hbm, keys_ref, *refs):
    grad_refs, outs = refs[:shares], refs[shares:-6]
    ids_ref, slot_ref, dropped_ref, weight_ref, in_ref, sem = refs[-6:]
    share = grad_refs[0].shape[0]
    copies = [
        pltpu.make_async_copy(src, dst, sem.at[i])
        for i, (src, dst) in enumerate(
            (
                (ids_hbm, ids_ref),
                (slot_hbm, slot_ref),
                (dropped_hbm, dropped_ref),
                (weight_hbm, weight_ref),
                (in_hbm, in_ref),
                *((grad_hbm.at[pl.ds(i * share, share)], ref) for i, ref in enumerate(grad_refs)),
            )
        )
    ]
    for copy in copies:
        copy.start()
    me = lax.axis_index("expert")
    for copy in copies[:4]:
        copy.wait()
    ids = ids_ref[...]
    live = (ids < n_expert) & (dropped_ref[...] == 0)
    keys = jnp.where(live, (ids ^ me) * PAIR + slot_ref[...], -1)
    keys_ref[...] = keys
    weight = weight_ref[...]
    rows = sum(out.shape[0] for out in outs)
    tokens = keys.shape[1]
    own = jnp.zeros((rows, tokens), F32)
    scaled = jnp.zeros((rows, tokens), F32)
    for k, hit in enumerate(match_rows(keys, 0, rows)):
        own = jnp.where(hit, 1.0, own)
        scaled = jnp.where(hit, weight[k : k + 1, :], scaled)
    first = is_first((rows, tokens))
    pick_in = jnp.where(first, own, 0.0).astype(BF16)
    pick_grad = jnp.where(first, 0.0, own).astype(BF16)
    row_weight = jnp.sum(scaled, axis=1, keepdims=True)
    copies[4].wait()
    got = jnp.dot(pick_in, in_ref[...], preferred_element_type=F32)
    scale = jnp.where(is_first(row_weight.shape), 1.0, row_weight)
    for i, ref in enumerate(grad_refs):
        copies[5 + i].wait()
        pick = pick_grad[:, i * share : (i + 1) * share]
        got = got + jnp.dot(pick, ref[...], preferred_element_type=F32)
    got = (scale * got).astype(BF16)
    start = 0
    for out in outs:
        out[...] = got[start : start + out.shape[0], :]
        start += out.shape[0]


def gather(ids, slots, dropped, weight, inputs, grads, chips, apart, shares):
    tokens, width = inputs.shape
    ranks = ids.shape[0]
    sizes = [n for c in range(chips) for n in ([PAIR, PAIR] if c in apart else [2 * PAIR])]
    outs = pl.pallas_call(
        functools.partial(gather_kernel, 2 * chips, shares),
        out_shape=[jax.ShapeDtypeStruct((ranks, tokens), jnp.int32)]
        + [jax.ShapeDtypeStruct((tokens // shares, width), BF16)] * shares
        + [jax.ShapeDtypeStruct((n, width), BF16) for n in sizes],
        in_specs=[pl.BlockSpec(memory_space=pltpu.HBM)] * 6,
        out_specs=vmem(1 + shares + len(sizes)),
        scratch_shapes=[pltpu.VMEM((ranks, tokens), jnp.int32)] * 3
        + [pltpu.VMEM((ranks, tokens), F32)]
        + [pltpu.VMEM((tokens, width), BF16)]
        + [pltpu.SemaphoreType.DMA((5 + shares,))],
        name="gather",
        compiler_params=pltpu.CompilerParams(vmem_limit_bytes=16 << 20),
        cost_estimate=SHORT,
    )(*pinned((ids, slots, dropped, weight, inputs, grads)))
    keys, held, outs = outs[0], outs[1 : 1 + shares], list(outs[1 + shares :])
    return keys, held, [[outs.pop(0), outs.pop(0)] if c in apart else outs.pop(0) for c in range(chips)]


def load_kernel(gate_hbm, up_hbm, down_hbm, both_ref, down_ref, sem):
    hidden = gate_hbm.shape[1]
    copies = [
        pltpu.make_async_copy(gate_hbm, both_ref.at[:, :hidden], sem.at[0]),
        pltpu.make_async_copy(up_hbm, both_ref.at[:, hidden:], sem.at[1]),
        pltpu.make_async_copy(down_hbm, down_ref, sem.at[2]),
    ]
    for copy in copies:
        copy.start()
    for copy in copies:
        copy.wait()


def pinned(arrays):
    return [pltpu.with_memory_space_constraint(a, pltpu.HBM) for a in arrays]


def load(w_gate, w_up, w_down):
    width, hidden = w_gate.shape
    return pl.pallas_call(
        load_kernel,
        out_shape=[
            jax.ShapeDtypeStruct((width, 2 * hidden), BF16),
            jax.ShapeDtypeStruct((hidden, width), BF16),
        ],
        in_specs=[pl.BlockSpec(memory_space=pltpu.HBM)] * 3,
        out_specs=vmem(2),
        scratch_shapes=[pltpu.SemaphoreType.DMA((3,))],
        name="load",
        compiler_params=pltpu.CompilerParams(vmem_limit_bytes=12 << 20),
        cost_estimate=SHORT,
    )(*pinned((w_gate, w_up, w_down)))


def nt(a, b):
    return lax.dot_general(a, b, (((1,), (1,)), ((), ())), preferred_element_type=F32)


def tn(a, b):
    return lax.dot_general(a, b, (((0,), (0,)), ((), ())), preferred_element_type=F32)


def joined(refs, spans):
    return jnp.concatenate([r[lo:hi, :] for r, (lo, hi) in zip(refs, spans)], axis=0)


def expert_kernel(spans, with_keys, *refs):
    count = len(spans)
    if with_keys:
        keys_ref, refs = refs[0], refs[1:]
    payloads = refs[:count]
    w_both, w_down = refs[count : count + 2]
    returns = refs[count + 2 : -2]
    grads_out, hidden_out = refs[-2:]
    rows = sum(hi - lo for lo, hi in spans)
    width, units = w_down.shape[1], w_down.shape[0]
    half = width // 2
    both = joined(payloads, spans)
    pre = jnp.dot(both, w_both[...], preferred_element_type=F32)
    gate_pre, up_pre = pre[:, :units], pre[:, units:]
    hidden_grad = pltpu.roll(nt(both, w_down[...]), rows - CAP, 0)
    first = is_first(gate_pre.shape)
    sigma = jax.nn.sigmoid(gate_pre)
    active = gate_pre * sigma
    hidden = jnp.where(first, active * up_pre, 0.0)
    gate_grad = hidden_grad * up_pre * sigma * (1.0 + gate_pre * (1.0 - sigma))
    gate_grad = jnp.where(first, gate_grad, 0.0)
    up_grad = jnp.where(first, hidden_grad * active, 0.0)
    grads = jnp.concatenate([gate_grad, up_grad], axis=1)
    grads_two = (grads + pltpu.roll(grads, CAP, 0)).astype(BF16)
    left = nt(grads_two, w_both[:half, :])
    right = nt(grads_two, w_both[half:, :])
    row_grad = jnp.where(is_first(left.shape), left, right).astype(BF16)
    step = rows // len(returns)
    for k, out in enumerate(returns):
        out[:step, :] = row_grad[k * step : (k + 1) * step, :]
    grads_out[...] = grads.astype(BF16)
    hidden_out[...] = pltpu.roll(hidden, CAP, 0).astype(BF16)
    if with_keys:
        ranks, tokens = keys_ref.shape
        keys = keys_ref[...].astype(F32)
        block = jnp.floor((keys + 0.5) / PAIR)
        for out in returns:
            out[2 * PAIR :, :tokens] = block.astype(BF16)
            out[2 * PAIR :, tokens : 2 * tokens] = (keys - PAIR * block).astype(BF16)
            out[2 * PAIR :, 2 * tokens :] = jnp.zeros((ranks, half - 2 * tokens), BF16)


def expert_chunk(pieces, w_both, w_down, keys=None):
    arrays, spans = [p[0] for p in pieces], [p[1] for p in pieces]
    total = sum(hi - lo for lo, hi in spans)
    hidden, width = w_down.shape
    extra = [] if keys is None else [keys]
    rows = [2 * PAIR] * (total // (2 * PAIR))
    if extra:
        rows = [r + keys.shape[0] for r in rows]
    out = pl.pallas_call(
        functools.partial(expert_kernel, spans, bool(extra)),
        out_shape=[jax.ShapeDtypeStruct((r, width // 2), BF16) for r in rows]
        + [jax.ShapeDtypeStruct((total, n * hidden), BF16) for n in (2, 1)],
        in_specs=vmem(len(extra) + len(pieces) + 2),
        out_specs=vmem(len(rows) + 2),
        name="expert",
        compiler_params=pltpu.CompilerParams(vmem_limit_bytes=20 << 20),
        cost_estimate=SHORT,
    )(*extra, *arrays, w_both, w_down)
    return out[: len(rows)], out[len(rows) :]


def weight_kernel(spans, chunks, *refs):
    count = len(spans)
    payloads = refs[:count]
    small = refs[count : count + 2 * chunks]
    grad_gate, grad_up, grad_down = refs[count + 2 * chunks :]
    units = grad_gate.shape[1]
    both = joined(payloads, spans)
    grads = jnp.concatenate([r[...] for r in small[0::2]], axis=0)
    hidden = jnp.concatenate([r[...] for r in small[1::2]], axis=0)
    made = tn(both, grads).astype(BF16)
    grad_gate[...] = made[:, :units]
    grad_up[...] = made[:, units:]
    grad_down[...] = tn(hidden, both).astype(BF16)


def weight_grads(pieces, small, width, hidden):
    count = len(pieces)
    payloads, spans = [p[0] for p in pieces], [p[1] for p in pieces]
    chunks = len(small)
    flat = [a for part in small for a in part]
    return pl.pallas_call(
        functools.partial(weight_kernel, spans, chunks),
        out_shape=[
            jax.ShapeDtypeStruct((width, hidden), BF16),
            jax.ShapeDtypeStruct((width, hidden), BF16),
            jax.ShapeDtypeStruct((hidden, width), BF16),
        ],
        in_specs=vmem(count + 2 * chunks),
        out_specs=vmem(3),
        name="weight_grads",
        compiler_params=pltpu.CompilerParams(vmem_limit_bytes=24 << 20),
        cost_estimate=SHORT,
    )(*payloads, *flat)


def combine_kernel(spans, start, ranks, bases, keys_ref, *refs):
    base_refs, returned = refs[:bases], refs[bases : bases + len(spans)]
    out, *scratch = refs[bases + len(spans) :]
    rows = sum(hi - lo for lo, hi in spans)
    share = base_refs[0].shape[0]
    tokens, width = out.shape
    block = keys_ref[2 * PAIR : 2 * PAIR + ranks, :tokens].astype(F32)
    slot = keys_ref[2 * PAIR : 2 * PAIR + ranks, tokens : 2 * tokens].astype(F32)
    keys = (PAIR * block + slot).astype(jnp.int32)
    own = jnp.zeros((rows, tokens), F32)
    for hit in match_rows(keys, start * PAIR, rows):
        own = jnp.where(hit, 1.0, own)
    first = is_first((rows, tokens))
    picks = [jnp.where(first, own, 0.0).astype(BF16), jnp.where(first, 0.0, own).astype(BF16)]
    back = joined(returned, spans)
    quarter = width // 4
    copies = []
    for i in range(4):
        cols = slice(i * quarter, (i + 1) * quarter)
        side = slice(i % 2 * quarter, (i % 2 + 1) * quarter)
        added = tn(picks[i // 2], back[:, side])
        for j, ref in enumerate(base_refs):
            here = slice(j * share, (j + 1) * share)
            total = ref[:, cols].astype(F32) + added[here, :]
            (scratch[0] if scratch else out)[here, cols] = total.astype(out.dtype)
        if scratch:
            copy = pltpu.make_async_copy(scratch[0].at[:, cols], out.at[:, cols], scratch[1].at[i])
            copy.start()
            copies.append(copy)
    for copy in copies:
        copy.wait()


def combine(ranks, carrier, bases, start, pieces, last):
    returned, spans = [p[0] for p in pieces], [p[1] for p in pieces]
    shape = (len(bases) * bases[0].shape[0], bases[0].shape[1])
    space = pltpu.HBM if last else pltpu.VMEM
    return pl.pallas_call(
        functools.partial(combine_kernel, spans, start, ranks, len(bases)),
        out_shape=jax.ShapeDtypeStruct(shape, BF16 if last else F32),
        in_specs=vmem(1 + len(bases) + len(returned)),
        out_specs=pl.BlockSpec(memory_space=space),
        scratch_shapes=[pltpu.VMEM(shape, BF16), pltpu.SemaphoreType.DMA((4,))] if last else [],
        name="combine",
        compiler_params=pltpu.CompilerParams(vmem_limit_bytes=16 << 20),
        cost_estimate=SHORT,
    )(carrier, *bases, *returned)


def per_device(
    tokens_in,
    out_grad,
    route_weight,
    expert_ids,
    slot_pos,
    dropped,
    gate_weight,
    up_weight,
    down_weight,
):
    inputs = tokens_in[0]
    grads = out_grad[0]
    w_gate = gate_weight[0, 0]
    w_up = up_weight[0, 0]
    w_down = down_weight[0, 0]
    width, hidden = w_gate.shape
    n_expert = lax.axis_size("expert")
    n_pipe = lax.axis_size("pipe")
    both_axes = ("pipe", "expert")

    def to_partner(value, k):
        return lax.ppermute(value, "expert", [(i, i ^ k) for i in range(n_expert)])

    def to_before(value, k):
        pairs = [
            (p * n_expert + i, (p - 1) * n_expert + (i ^ k))
            for p in range(1, n_pipe)
            for i in range(n_expert)
        ]
        return lax.ppermute(value, both_axes, pairs)

    chips = n_expert // 2
    near = list(range(1, chips // 2))
    early = list(range(chips // 2, 3 * chips // 4))
    late = list(range(3 * chips // 4, chips))
    by_rank = [jnp.transpose(a[0]) for a in (expert_ids, slot_pos, dropped, route_weight)]
    keys, held, sent = gather(*by_rank, inputs, grads, chips, [0] + late, SHARES)
    mine = (0, PAIR)

    def after(values, event):
        return lax.optimization_barrier((values, event))[0]

    def forward(value, *cuts):
        edges = [PAIR, *cuts, 2 * PAIR]
        pieces = [(value, mine)]
        for lo, hi in zip(edges, edges[1:]):
            pieces.append((to_partner(value[lo:hi], 1), (0, hi - lo)))
        return pieces

    def gated(pieces, event):
        values = after([p[0] for p in pieces], event)
        return [(v, p[1]) for v, p in zip(values, pieces)]

    arrived, order, small, returned = {}, [], [], {}

    def process(chunk, pieces, **options):
        back, parts = expert_chunk(pieces, w_both, w_down, **options)
        order.extend(pieces)
        small.append(parts)
        for c, value in zip(chunk, back):
            returned[c] = to_before(value, 2 * c)
        return parts

    for c in early + near:
        arrived[c] = to_partner(sent[c], 2 * c)
    for c in late:
        arrived[c] = [(to_partner(v, 2 * c + i), mine) for i, v in enumerate(sent[c])]
    beside = to_partner(sent[0][1], 1)
    next_grads = [to_before(share, 0) for share in held]
    pieces = [(sent[0][0], mine), (beside, mine)]
    w_both, w_down = load(*after((w_gate, w_up, w_down), sent[0][0]))
    here = after([arrived[c] for c in near], w_down)
    for value in here:
        pieces += forward(value)
    parts = process([0] + near, pieces, keys=keys)
    pieces = [piece for c in early for piece in forward(arrived[c], PAIR + 24)]
    parts = process(early, gated(pieces, (parts, next_grads[0])))
    pieces = [piece for c in late for piece in arrived[c]]
    process(late, gated(pieces, (parts, next_grads)))
    small[0] = after(small[0], [returned[c] for c in [0] + near])
    grad_gate, grad_up, grad_down = weight_grads(order, small, width, hidden)
    carrier = returned[0]
    pieces = []
    for c in range(chips):
        value = after(returned[c], grad_gate) if c not in late else returned[c]
        pieces += forward(value)
    upstream = combine(keys.shape[0], carrier, next_grads, 0, pieces, True)
    return (upstream[None], grad_gate[None, None], grad_up[None, None], grad_down[None, None])


def solution(mesh):
    return jax.shard_map(
        per_device,
        mesh=mesh,
        in_specs=(
            P("pipe", "expert", None),
            P("pipe", "expert", None),
            P("pipe", "expert", None),
            P("pipe", "expert", None),
            P("pipe", "expert", None),
            P("pipe", "expert", None),
            P("pipe", "expert", None, None),
            P("pipe", "expert", None, None),
            P("pipe", "expert", None, None),
        ),
        out_specs=(
            P("pipe", "expert", None),
            P("pipe", "expert", None, None),
            P("pipe", "expert", None, None),
            P("pipe", "expert", None, None),
        ),
        check_vma=False,
    )
```

```python
import functools

import jax
import jax.numpy as jnp
from jax import lax
from jax.experimental import pallas as pl
from jax.experimental.pallas import tpu as pltpu
from jax.sharding import PartitionSpec as P

CAP = 20
PAIR = 2 * CAP
SHARES = 1
F32 = jnp.float32
BF16 = jnp.bfloat16
SHORT = pl.CostEstimate(flops=1, transcendentals=0, bytes_accessed=1)


def vmem(count):
    return [pl.BlockSpec(memory_space=pltpu.VMEM)] * count


def is_first(shape):
    return lax.rem(lax.broadcasted_iota(jnp.int32, shape, 0), PAIR) < CAP


def match_rows(keys, first_row, rows):
    tokens = keys.shape[1]
    row = lax.broadcasted_iota(jnp.int32, (rows, tokens), 0)
    slot = first_row + row - jnp.where(lax.rem(row, PAIR) < CAP, 0, CAP)
    return [keys[k : k + 1, :] == slot for k in range(keys.shape[0])]


def gather_kernel(n_expert, shares, ids_hbm, slot_hbm, dropped_hbm, weight_hbm, in_hbm, grad_hbm, keys_ref, *refs):
    grad_refs, outs = refs[:shares], refs[shares:-6]
    ids_ref, slot_ref, dropped_ref, weight_ref, in_ref, sem = refs[-6:]
    share = grad_refs[0].shape[0]
    copies = [
        pltpu.make_async_copy(src, dst, sem.at[i])
        for i, (src, dst) in enumerate(
            (
                (ids_hbm, ids_ref),
                (slot_hbm, slot_ref),
                (dropped_hbm, dropped_ref),
                (weight_hbm, weight_ref),
                (in_hbm, in_ref),
                *((grad_hbm.at[pl.ds(i * share, share)], ref) for i, ref in enumerate(grad_refs)),
            )
        )
    ]
    for copy in copies:
        copy.start()
    me = lax.axis_index("expert")
    for copy in copies[:4]:
        copy.wait()
    ids = ids_ref[...]
    live = (ids < n_expert) & (dropped_ref[...] == 0)
    keys = jnp.where(live, (ids ^ me) * PAIR + slot_ref[...], -1)
    keys_ref[...] = keys
    weight = weight_ref[...]
    rows = sum(out.shape[0] for out in outs)
    tokens = keys.shape[1]
    own = jnp.zeros((rows, tokens), F32)
    scaled = jnp.zeros((rows, tokens), F32)
    for k, hit in enumerate(match_rows(keys, 0, rows)):
        own = jnp.where(hit, 1.0, own)
        scaled = jnp.where(hit, weight[k : k + 1, :], scaled)
    first = is_first((rows, tokens))
    pick_in = jnp.where(first, own, 0.0).astype(BF16)
    pick_grad = jnp.where(first, 0.0, own).astype(BF16)
    row_weight = jnp.sum(scaled, axis=1, keepdims=True)
    copies[4].wait()
    got = jnp.dot(pick_in, in_ref[...], preferred_element_type=F32)
    scale = jnp.where(is_first(row_weight.shape), 1.0, row_weight)
    for i, ref in enumerate(grad_refs):
        copies[5 + i].wait()
        pick = pick_grad[:, i * share : (i + 1) * share]
        got = got + jnp.dot(pick, ref[...], preferred_element_type=F32)
    got = (scale * got).astype(BF16)
    start = 0
    for out in outs:
        out[...] = got[start : start + out.shape[0], :]
        start += out.shape[0]


def gather(ids, slots, dropped, weight, inputs, grads, chips, apart, shares):
    tokens, width = inputs.shape
    ranks = ids.shape[0]
    sizes = [n for c in range(chips) for n in ([PAIR, PAIR] if c in apart else [2 * PAIR])]
    outs = pl.pallas_call(
        functools.partial(gather_kernel, 2 * chips, shares),
        out_shape=[jax.ShapeDtypeStruct((ranks, tokens), jnp.int32)]
        + [jax.ShapeDtypeStruct((tokens // shares, width), BF16)] * shares
        + [jax.ShapeDtypeStruct((n, width), BF16) for n in sizes],
        in_specs=[pl.BlockSpec(memory_space=pltpu.HBM)] * 6,
        out_specs=vmem(1 + shares + len(sizes)),
        scratch_shapes=[pltpu.VMEM((ranks, tokens), jnp.int32)] * 3
        + [pltpu.VMEM((ranks, tokens), F32)]
        + [pltpu.VMEM((tokens, width), BF16)]
        + [pltpu.SemaphoreType.DMA((5 + shares,))],
        name="gather",
        compiler_params=pltpu.CompilerParams(vmem_limit_bytes=16 << 20),
        cost_estimate=SHORT,
    )(*pinned((ids, slots, dropped, weight, inputs, grads)))
    keys, held, outs = outs[0], outs[1 : 1 + shares], list(outs[1 + shares :])
    return keys, held, [[outs.pop(0), outs.pop(0)] if c in apart else outs.pop(0) for c in range(chips)]


def load_kernel(gate_hbm, up_hbm, down_hbm, both_ref, back_ref, down_ref, held_ref, sem):
    hidden = gate_hbm.shape[1]
    copies = [
        pltpu.make_async_copy(gate_hbm, both_ref.at[:, :hidden], sem.at[0]),
        pltpu.make_async_copy(up_hbm, both_ref.at[:, hidden:], sem.at[1]),
        pltpu.make_async_copy(down_hbm, held_ref, sem.at[2]),
    ]
    for copy in copies:
        copy.start()
    for copy in copies:
        copy.wait()
    down_ref[...] = held_ref[...].T
    back_ref[...] = both_ref[...].T


def pinned(arrays):
    return [pltpu.with_memory_space_constraint(a, pltpu.HBM) for a in arrays]


def load(w_gate, w_up, w_down):
    width, hidden = w_gate.shape
    return pl.pallas_call(
        load_kernel,
        out_shape=[
            jax.ShapeDtypeStruct((width, 2 * hidden), BF16),
            jax.ShapeDtypeStruct((2 * hidden, width), BF16),
            jax.ShapeDtypeStruct((width, hidden), BF16),
        ],
        in_specs=[pl.BlockSpec(memory_space=pltpu.HBM)] * 3,
        out_specs=vmem(3),
        scratch_shapes=[pltpu.VMEM((hidden, width), BF16), pltpu.SemaphoreType.DMA((3,))],
        name="load",
        compiler_params=pltpu.CompilerParams(vmem_limit_bytes=24 << 20),
        cost_estimate=SHORT,
    )(*pinned((w_gate, w_up, w_down)))


def nt(a, b):
    return lax.dot_general(a, b, (((1,), (1,)), ((), ())), preferred_element_type=F32)


def tn(a, b):
    return lax.dot_general(a, b, (((0,), (0,)), ((), ())), preferred_element_type=F32)


def joined(refs, spans):
    return jnp.concatenate([r[lo:hi, :] for r, (lo, hi) in zip(refs, spans)], axis=0)


def expert_kernel(spans, with_keys, *refs):
    count = len(spans)
    if with_keys:
        keys_ref, refs = refs[0], refs[1:]
    payloads = refs[:count]
    w_both, w_back, w_down = refs[count : count + 3]
    returns = refs[count + 3 : -2]
    grads_out, hidden_out = refs[-2:]
    rows = sum(hi - lo for lo, hi in spans)
    width, units = w_down.shape
    half = width // 2
    both = joined(payloads, spans)
    pre = jnp.dot(both, w_both[...], preferred_element_type=F32)
    gate_pre, up_pre = pre[:, :units], pre[:, units:]
    hidden_grad = pltpu.roll(jnp.dot(both, w_down[...], preferred_element_type=F32), rows - CAP, 0)
    first = is_first(gate_pre.shape)
    sigma = jax.nn.sigmoid(gate_pre)
    active = gate_pre * sigma
    hidden = jnp.where(first, active * up_pre, 0.0)
    gate_grad = hidden_grad * up_pre * sigma * (1.0 + gate_pre * (1.0 - sigma))
    gate_grad = jnp.where(first, gate_grad, 0.0)
    up_grad = jnp.where(first, hidden_grad * active, 0.0)
    grads = jnp.concatenate([gate_grad, up_grad], axis=1)
    grads_two = (grads + pltpu.roll(grads, CAP, 0)).astype(BF16)
    left = jnp.dot(grads_two, w_back[:, :half], preferred_element_type=F32)
    right = jnp.dot(grads_two, w_back[:, half:], preferred_element_type=F32)
    row_grad = jnp.where(is_first(left.shape), left, right).astype(BF16)
    step = rows // len(returns)
    for k, out in enumerate(returns):
        out[:step, :] = row_grad[k * step : (k + 1) * step, :]
    grads_out[...] = grads.astype(BF16)
    hidden_out[...] = pltpu.roll(hidden, CAP, 0).astype(BF16)
    if with_keys:
        ranks, tokens = keys_ref.shape
        keys = keys_ref[...].astype(F32)
        block = jnp.floor((keys + 0.5) / PAIR)
        for out in returns:
            out[2 * PAIR :, :tokens] = block.astype(BF16)
            out[2 * PAIR :, tokens : 2 * tokens] = (keys - PAIR * block).astype(BF16)
            out[2 * PAIR :, 2 * tokens :] = jnp.zeros((ranks, half - 2 * tokens), BF16)


def expert_chunk(pieces, weights, keys=None):
    arrays, spans = [p[0] for p in pieces], [p[1] for p in pieces]
    total = sum(hi - lo for lo, hi in spans)
    width, hidden = weights[2].shape
    extra = [] if keys is None else [keys]
    rows = [2 * PAIR] * (total // (2 * PAIR))
    if extra:
        rows = [r + keys.shape[0] for r in rows]
    out = pl.pallas_call(
        functools.partial(expert_kernel, spans, bool(extra)),
        out_shape=[jax.ShapeDtypeStruct((r, width // 2), BF16) for r in rows]
        + [jax.ShapeDtypeStruct((total, n * hidden), BF16) for n in (2, 1)],
        in_specs=vmem(len(extra) + len(pieces) + 3),
        out_specs=vmem(len(rows) + 2),
        name="expert",
        compiler_params=pltpu.CompilerParams(vmem_limit_bytes=20 << 20),
        cost_estimate=SHORT,
    )(*extra, *arrays, *weights)
    return out[: len(rows)], out[len(rows) :]


def weight_kernel(spans, chunks, *refs):
    count = len(spans)
    payloads = refs[:count]
    small = refs[count : count + 2 * chunks]
    grad_gate, grad_up, grad_down = refs[count + 2 * chunks :]
    units = grad_gate.shape[1]
    both = joined(payloads, spans)
    grads = jnp.concatenate([r[...] for r in small[0::2]], axis=0)
    hidden = jnp.concatenate([r[...] for r in small[1::2]], axis=0)
    made = tn(both, grads).astype(BF16)
    grad_gate[...] = made[:, :units]
    grad_up[...] = made[:, units:]
    grad_down[...] = tn(hidden, both).astype(BF16)


def weight_grads(pieces, small, width, hidden):
    count = len(pieces)
    payloads, spans = [p[0] for p in pieces], [p[1] for p in pieces]
    chunks = len(small)
    flat = [a for part in small for a in part]
    return pl.pallas_call(
        functools.partial(weight_kernel, spans, chunks),
        out_shape=[
            jax.ShapeDtypeStruct((width, hidden), BF16),
            jax.ShapeDtypeStruct((width, hidden), BF16),
            jax.ShapeDtypeStruct((hidden, width), BF16),
        ],
        in_specs=vmem(count + 2 * chunks),
        out_specs=vmem(3),
        name="weight_grads",
        compiler_params=pltpu.CompilerParams(vmem_limit_bytes=24 << 20),
        cost_estimate=SHORT,
    )(*payloads, *flat)


def combine_kernel(spans, start, ranks, bases, keys_ref, *refs):
    base_refs, returned = refs[:bases], refs[bases : bases + len(spans)]
    out, *scratch = refs[bases + len(spans) :]
    rows = sum(hi - lo for lo, hi in spans)
    share = base_refs[0].shape[0]
    tokens, width = out.shape
    block = keys_ref[2 * PAIR : 2 * PAIR + ranks, :tokens].astype(F32)
    slot = keys_ref[2 * PAIR : 2 * PAIR + ranks, tokens : 2 * tokens].astype(F32)
    keys = (PAIR * block + slot).astype(jnp.int32)
    own = jnp.zeros((rows, tokens), F32)
    for hit in match_rows(keys, start * PAIR, rows):
        own = jnp.where(hit, 1.0, own)
    first = is_first((rows, tokens))
    picks = [jnp.where(first, own, 0.0).astype(BF16), jnp.where(first, 0.0, own).astype(BF16)]
    back = joined(returned, spans)
    quarter = width // 4
    copies = []
    for i in range(4):
        cols = slice(i * quarter, (i + 1) * quarter)
        side = slice(i % 2 * quarter, (i % 2 + 1) * quarter)
        added = tn(picks[i // 2], back[:, side])
        for j, ref in enumerate(base_refs):
            here = slice(j * share, (j + 1) * share)
            total = ref[:, cols].astype(F32) + added[here, :]
            (scratch[0] if scratch else out)[here, cols] = total.astype(out.dtype)
        if scratch:
            copy = pltpu.make_async_copy(scratch[0].at[:, cols], out.at[:, cols], scratch[1].at[i])
            copy.start()
            copies.append(copy)
    for copy in copies:
        copy.wait()


def combine(ranks, carrier, bases, start, pieces, last):
    returned, spans = [p[0] for p in pieces], [p[1] for p in pieces]
    shape = (len(bases) * bases[0].shape[0], bases[0].shape[1])
    space = pltpu.HBM if last else pltpu.VMEM
    return pl.pallas_call(
        functools.partial(combine_kernel, spans, start, ranks, len(bases)),
        out_shape=jax.ShapeDtypeStruct(shape, BF16 if last else F32),
        in_specs=vmem(1 + len(bases) + len(returned)),
        out_specs=pl.BlockSpec(memory_space=space),
        scratch_shapes=[pltpu.VMEM(shape, BF16), pltpu.SemaphoreType.DMA((4,))] if last else [],
        name="combine",
        compiler_params=pltpu.CompilerParams(vmem_limit_bytes=16 << 20),
        cost_estimate=SHORT,
    )(carrier, *bases, *returned)


def per_device(
    tokens_in,
    out_grad,
    route_weight,
    expert_ids,
    slot_pos,
    dropped,
    gate_weight,
    up_weight,
    down_weight,
):
    inputs = tokens_in[0]
    grads = out_grad[0]
    w_gate = gate_weight[0, 0]
    w_up = up_weight[0, 0]
    w_down = down_weight[0, 0]
    width, hidden = w_gate.shape
    n_expert = lax.axis_size("expert")
    n_pipe = lax.axis_size("pipe")
    both_axes = ("pipe", "expert")

    def to_partner(value, k):
        return lax.ppermute(value, "expert", [(i, i ^ k) for i in range(n_expert)])

    def to_before(value, k):
        pairs = [
            (p * n_expert + i, (p - 1) * n_expert + (i ^ k))
            for p in range(1, n_pipe)
            for i in range(n_expert)
        ]
        return lax.ppermute(value, both_axes, pairs)

    chips = n_expert // 2
    near = list(range(1, chips // 2))
    early = list(range(chips // 2, 3 * chips // 4))
    late = list(range(3 * chips // 4, chips))
    by_rank = [jnp.transpose(a[0]) for a in (expert_ids, slot_pos, dropped, route_weight)]
    keys, held, sent = gather(*by_rank, inputs, grads, chips, [0] + late, SHARES)
    mine = (0, PAIR)

    def after(values, event):
        return lax.optimization_barrier((values, event))[0]

    def forward(value, *cuts):
        edges = [PAIR, *cuts, 2 * PAIR]
        pieces = [(value, mine)]
        for lo, hi in zip(edges, edges[1:]):
            pieces.append((to_partner(value[lo:hi], 1), (0, hi - lo)))
        return pieces

    def gated(pieces, event):
        values = after([p[0] for p in pieces], event)
        return [(v, p[1]) for v, p in zip(values, pieces)]

    arrived, order, small, returned = {}, [], [], {}

    def process(chunk, pieces, **options):
        back, parts = expert_chunk(pieces, turned, **options)
        order.extend(pieces)
        small.append(parts)
        for c, value in zip(chunk, back):
            returned[c] = to_before(value, 2 * c)
        return parts

    for c in early + near:
        arrived[c] = to_partner(sent[c], 2 * c)
    for c in late:
        arrived[c] = [(to_partner(v, 2 * c + i), mine) for i, v in enumerate(sent[c])]
    beside = to_partner(sent[0][1], 1)
    next_grads = [to_before(share, 0) for share in held]
    pieces = [(sent[0][0], mine), (beside, mine)]
    turned = load(*after((w_gate, w_up, w_down), sent[0][0]))
    here = after([arrived[c] for c in near], turned)
    for value in here:
        pieces += forward(value)
    parts = process([0] + near, pieces, keys=keys)
    pieces = [piece for c in early for piece in forward(arrived[c], PAIR + 24)]
    parts = process(early, gated(pieces, parts))
    pieces = [piece for c in late for piece in arrived[c]]
    process(late, gated(pieces, (parts, next_grads)))
    small[0] = after(small[0], [returned[c] for c in [0] + near])
    grad_gate, grad_up, grad_down = weight_grads(order, small, width, hidden)
    carrier = returned[0]
    pieces = []
    for c in range(chips):
        value = after(returned[c], grad_gate) if c not in late else returned[c]
        pieces += forward(value)
    upstream = combine(keys.shape[0], carrier, next_grads, 0, pieces, True)
    return (upstream[None], grad_gate[None, None], grad_up[None, None], grad_down[None, None])


def solution(mesh):
    return jax.shard_map(
        per_device,
        mesh=mesh,
        in_specs=(
            P("pipe", "expert", None),
            P("pipe", "expert", None),
            P("pipe", "expert", None),
            P("pipe", "expert", None),
            P("pipe", "expert", None),
            P("pipe", "expert", None),
            P("pipe", "expert", None, None),
            P("pipe", "expert", None, None),
            P("pipe", "expert", None, None),
        ),
        out_specs=(
            P("pipe", "expert", None),
            P("pipe", "expert", None, None),
            P("pipe", "expert", None, None),
            P("pipe", "expert", None, None),
        ),
        check_vma=False,
    )
```
